128 devices in a mesh: dp: 16 (over x, y_hi, core), mp: 8 (over y_lo, z).
Axes of the slice: x: 4, y: 4 (y_hi: 2, y_lo: 2; y = y_hi * 2 + y_lo), z: 4, core: 2. Of those that a mesh axis runs over, the one named last changes fastest.
Arguments:
- clean_image: bfloat16 [8, 588, 128], P('mp'), may hold values from -6 to 6
- noise_draw: bfloat16 [8, 16, 588, 128], P('mp', 'dp'), may hold values from -6 to 6
- embed_weight: bfloat16 [588, 6144], P(None, 'dp'), may hold values from -0.25 to 0.25
- position_table: bfloat16 [128, 6144], replicated, may hold values from -3 to 3
- norm_gain: float32 [6144], replicated, may hold values from 0.1 to 1.9
- qkv_weight: bfloat16 [6144, 3, 3072], P(None, None, 'mp'), may hold values from -0.078125 to 0.078125
- query_gain: float32 [128], replicated, may hold values from 0.1 to 1.9
- key_gain: float32 [128], replicated, may hold values from 0.1 to 1.9
- out_weight: bfloat16 [3072, 6144], P('mp'), may hold values from -0.375 to 0.375
Outputs:
- features: bfloat16 [128, 16, 8, 6144], P(None, 'dp', 'mp')
- smoothed: float32 [128, 8, 6144], P(None, 'mp', 'dp')
The draws below stay inside these ranges and needn't reach their ends.
All inputs are finite; a program needn't handle non-finite values.
Results may differ from the reference program's by a relative error of at most 0.017.
Values may be sent and summed in bfloat16 or wider, within the bound.
No kernel may reach another device: no remote copies, remote signals or barrier semaphores. Data moves between devices by JAX's collectives and lax.ppermute only.
A program may use at most 128 MiB of HBM per device.

```python
import jax
import jax.numpy as jnp
from jax import lax

D = 6144
HEAD_DIM = 128
PIX = 588
HEADS = 24
PATCHES = 128
IMAGES = 8
COPIES = 16
N_MP = 8


def shard_levels(stream_key, dims, split, least, largest):
    def one(position, blocks):
        draws = jax.random.uniform(jax.random.fold_in(jax.random.fold_in(stream_key, 6), position), (blocks,), jnp.float32, least / len(split), largest / len(split))
        return jnp.repeat(jnp.exp(draws), dims[position] // blocks).reshape((-1,) + (1,) * (len(dims) - position - 1))

    level = one(*split[0])
    for cut in split[1:]:
        level = level * one(*cut)
    return level


def scatter_about(key, dims, scale, limit, shards=(), dtype=jnp.bfloat16):
    drawn = scale * jax.random.normal(key, dims, jnp.float32)
    if shards:
        drawn = drawn * shard_levels(key, dims, shards, -0.22, 0.18)
    return jnp.clip(drawn, -limit, limit).astype(dtype)


def setup_inputs(seed: int = 0) -> dict:
    key_list = jax.random.split(jax.random.key(seed), 10)
    return {
        "clean_image": scatter_about(key_list[0], (IMAGES, PIX, PATCHES), 1.0, 6.0, ((0, 8),)),
        "noise_draw": scatter_about(key_list[1], (IMAGES, COPIES, PIX, PATCHES), 1.0, 6.0, ((0, 8), (1, 16))),
        "embed_weight": scatter_about(key_list[2], (PIX, D), PIX ** -0.5, 0.25, ((1, 16),)),
        "position_table": scatter_about(key_list[3], (PATCHES, D), 0.5, 3.0),
        "norm_gain": jnp.clip(1.0 + 0.18 * jax.random.normal(key_list[4], (D,), jnp.float32), 0.1, 1.9),
        "qkv_weight": scatter_about(key_list[5], (D, 3, HEADS * HEAD_DIM), D ** -0.5, 0.078125, ((2, 8),)),
        "query_gain": jnp.clip(1.0 + 0.18 * jax.random.normal(key_list[6], (HEAD_DIM,), jnp.float32), 0.1, 1.9),
        "key_gain": jnp.clip(1.0 + 0.18 * jax.random.normal(key_list[7], (HEAD_DIM,), jnp.float32), 0.1, 1.9),
        "out_weight": scatter_about(key_list[8], (HEADS * HEAD_DIM, D), (2 * HEAD_DIM) ** -0.5, 0.375, ((0, 8),)),
    }


epsilon = 1e-06

def layer_norm(values, gain_vec):
    average = lax.optimization_barrier(jnp.mean(values, axis=-1, keepdims=True))
    centred = values - average
    variance = lax.optimization_barrier(jnp.mean(centred * centred, axis=-1, keepdims=True))
    return centred * lax.rsqrt(variance + epsilon) * gain_vec

def reference(clean_image, noise_draw, embed_weight, position_table, norm_gain, qkv_weight, query_gain, key_gain, out_weight):
    highest = lax.Precision.HIGHEST
    num_images = clean_image.shape[0]
    num_patches = clean_image.shape[2]
    num_copies = noise_draw.shape[1]
    width = embed_weight.shape[1]
    group = HEADS * HEAD_DIM // N_MP
    position_f = position_table.astype(jnp.float32)
    copies_first = jnp.moveaxis(noise_draw, 1, 0)

    def one_copy(carry, copy_noise):
        noisy_img = (clean_image.astype(jnp.float32) + 0.5 * copy_noise.astype(jnp.float32)).astype(jnp.bfloat16)
        embedded = jnp.einsum('ikp,kd->pid', noisy_img.astype(jnp.float32), embed_weight.astype(jnp.float32), precision=highest) + position_f[:, None, :]
        normed = layer_norm(embedded, norm_gain).astype(jnp.bfloat16)
        projected = jnp.einsum('pid,dtc->pitc', normed.astype(jnp.float32), qkv_weight.astype(jnp.float32), precision=highest)
        query = projected[:, :, 0].reshape(num_patches, num_images, HEADS, HEAD_DIM)
        key_vec = projected[:, :, 1].reshape(num_patches, num_images, HEADS, HEAD_DIM)
        value = projected[:, :, 2].reshape(num_patches, num_images, HEADS, HEAD_DIM).astype(jnp.bfloat16)
        query = layer_norm(query, query_gain).astype(jnp.bfloat16)
        key_vec = layer_norm(key_vec, key_gain).astype(jnp.bfloat16)
        scores = jnp.einsum('pihe,sihe->ihps', query.astype(jnp.float32), key_vec.astype(jnp.float32), precision=highest) * HEAD_DIM ** (-0.5)
        exp_scores = jnp.exp(scores)
        probs = (exp_scores / lax.optimization_barrier(jnp.sum(exp_scores, axis=-1, keepdims=True))).astype(jnp.bfloat16)
        head_out = jnp.einsum('ihps,sihe->pihe', probs.astype(jnp.float32), value.astype(jnp.float32), precision=highest)
        head_out = head_out.astype(jnp.bfloat16).reshape(num_patches, num_images, HEADS * HEAD_DIM)
        attention = jnp.zeros((num_patches, num_images, width), jnp.float32)
        for group_index in range(N_MP):
            lower = group_index * group
            partial_sum = jnp.einsum('pic,cd->pid', head_out[:, :, lower:lower + group].astype(jnp.float32), out_weight[lower:lower + group].astype(jnp.float32), precision=highest)
            partial_sum = lax.optimization_barrier(partial_sum.astype(jnp.bfloat16)).astype(jnp.float32)
            attention = attention + partial_sum
        output = embedded + attention
        carry = carry + output * (1.0 / num_copies)
        return (carry, output.astype(jnp.bfloat16))
    start_sum = jnp.zeros((num_patches, num_images, width), jnp.float32)
    smoothed, stacked = lax.scan(one_copy, start_sum, copies_first)
    features = jnp.moveaxis(stacked, 0, 1)
    return (features, smoothed)
```

```python
import jax
import jax.numpy as jnp
from jax import lax
from jax.sharding import Mesh
from jax.sharding import PartitionSpec as P

HEAD_DIM = 128
epsilon = 1e-06
bf16 = jnp.bfloat16
f32 = jnp.float32

AXES = ("x", "yh", "core", "yl", "z")
GROUP = ("x", "core")
DP = ("x", "yh", "core")
MP = ("yl", "z")
PIX_ROWS = 37
POS_ROWS = 8
ROWS = 48
PIECES = 16


def device_id(xc, yh, m):
    return (((xc // 2) * 2 + yh) * 2 + xc % 2) * 8 + m


def everyone():
    return [(xc, yh, m) for xc in range(8) for yh in range(2) for m in range(8)]


def send(array, target):
    pairs = [(device_id(*s), device_id(*target(*s))) for s in everyone()]
    return lax.ppermute(array, AXES, pairs)


def extended(pixel_rows, pos_rows):
    k, n = pixel_rows.shape
    pix = jnp.pad(pixel_rows, ((0, PIECES * PIX_ROWS - k), (0, 0))).reshape(PIECES, PIX_ROWS, n)
    pos = pos_rows.reshape(PIECES, POS_ROWS, n)
    spare = jnp.zeros((PIECES, ROWS - PIX_ROWS - POS_ROWS, n), pix.dtype)
    return jnp.concatenate([pix, pos, spare], axis=1)


def split_two(values):
    high = values.astype(bf16)
    return high, (values - high.astype(f32)).astype(bf16)


def head_norm(raw, scale, gain):
    average = jnp.mean(raw, axis=-1, keepdims=True)
    centred = raw - average
    variance = jnp.mean(centred * centred, axis=-1, keepdims=True)
    return centred * (scale * lax.rsqrt(variance * scale * scale + epsilon)) * gain


def on_device(
    clean_image,
    noise_draw,
    embed_weight,
    position_table,
    norm_gain,
    qkv_weight,
    query_gain,
    key_gain,
    out_weight,
):
    xi, yhi, ci = (lax.axis_index(a) for a in ("x", "yh", "core"))
    mi = lax.axis_index(MP)
    di = lax.axis_index(DP)
    patches, width = position_table.shape
    cols = embed_weight.shape[1]
    heads_here = qkv_weight.shape[2] // HEAD_DIM
    group_cols = qkv_weight.shape[2]

    def my_columns(array):
        blocks = array.reshape(array.shape[0], 4, 2, 2, cols)
        blocks = lax.dynamic_slice_in_dim(blocks, xi, 1, axis=1)
        return lax.dynamic_slice_in_dim(blocks, ci, 1, axis=3).reshape(array.shape[0], 2 * cols)

    out_all = lax.all_gather(my_columns(out_weight), MP)

    position_f = position_table.astype(f32)
    position_c = position_f - jnp.mean(position_f, axis=-1, keepdims=True)
    weight_f = embed_weight.astype(f32)
    local_mean = jnp.mean(weight_f, axis=-1, keepdims=True)
    gain_here = lax.dynamic_slice_in_dim(norm_gain, di * cols, cols, axis=0)
    centred_here = extended(
        ((weight_f - local_mean) * gain_here).astype(bf16),
        (lax.dynamic_slice_in_dim(position_c, di * cols, cols, axis=1) * gain_here).astype(bf16),
    ).reshape(PIECES * ROWS, cols)
    qkv_here = lax.dynamic_slice_in_dim(jnp.transpose(qkv_weight, (1, 0, 2)), di * cols, cols, axis=1)
    partial_sum = jnp.einsum("kd,tdc->tkc", centred_here, qkv_here, preferred_element_type=f32)
    partial_sum = partial_sum.astype(bf16).reshape(3, PIECES, ROWS, group_cols)
    col_sum = jnp.sum(qkv_here.astype(f32) * gain_here[None, :, None], axis=1)
    sum_high, sum_low = split_two(col_sum)
    mean_rows = jnp.pad(local_mean[:, 0], (0, PIECES * PIX_ROWS - local_mean.shape[0]))
    mean_rows = mean_rows.reshape(PIECES, PIX_ROWS)
    mean_high, mean_low = split_two(mean_rows)
    lanes = ((0, 0), (0, HEAD_DIM - PIX_ROWS))
    mean_line = jnp.concatenate(
        [jnp.pad(mean_high, lanes), jnp.pad(mean_low, lanes), jnp.zeros((PIECES, group_cols - 2 * HEAD_DIM), bf16)],
        axis=1,
    )
    lines = jnp.stack(
        [
            jnp.broadcast_to(sum_high[:, None], (3, PIECES, group_cols)),
            jnp.broadcast_to(sum_low[:, None], (3, PIECES, group_cols)),
            jnp.broadcast_to(mean_line[None], (3, PIECES, group_cols)),
        ],
        axis=2,
    )
    used = PIX_ROWS + POS_ROWS
    pieces = jnp.concatenate([partial_sum[:, :, :used], lines], axis=2)

    piece_here = (2 * xi + ci) * 2 + yhi

    def piece_of(k):
        return lax.dynamic_index_in_dim(pieces, piece_here ^ k, 1, keepdims=False)

    arrived = [piece_of(0)]
    for k in range(1, PIECES):
        arrived.append(send(piece_of(k), lambda xc, yh, m, k=k: (xc ^ (k >> 1), yh ^ (k & 1), m)))

    noisy = (clean_image[0].astype(f32) + 0.5 * noise_draw[0, 0].astype(f32)).astype(bf16)
    lhs_own = extended(noisy, jnp.eye(patches, dtype=bf16))
    lhs = lax.all_to_all(jnp.broadcast_to(lhs_own[None], (8, *lhs_own.shape)), GROUP, 0, 0, tiled=True)
    lhs = lhs.reshape(8, PIECES * ROWS, patches)

    other_weight = lax.ppermute(embed_weight, "yh", [(0, 1), (1, 0)])
    first, second = (
        jnp.where(yhi == 0, embed_weight, other_weight),
        jnp.where(yhi == 0, other_weight, embed_weight),
    )
    weight_two = extended(jnp.concatenate([first, second], axis=1), my_columns(position_table))
    weight_two = weight_two.reshape(PIECES * ROWS, 2 * cols)
    embedded = jnp.einsum("ckp,kd->cpd", lhs, weight_two, preferred_element_type=f32)

    average = jnp.mean(embedded, axis=-1)
    spread = jnp.mean(jnp.square(embedded - average[..., None]), axis=-1)
    stat = jnp.stack([average, spread])
    for bit in (1, 2, 4):
        other = send(stat, lambda xc, yh, m, bit=bit: (xc ^ bit, yh, m))
        gap = 0.5 * (stat[0] - other[0])
        stat = jnp.stack([0.5 * (stat[0] + other[0]), 0.5 * (stat[1] + other[1]) + gap * gap])
    scale = lax.rsqrt(stat[1] + epsilon)[..., None, None]

    arrived = jnp.stack(arrived)
    total = jnp.sum(arrived[:, :, :used].astype(f32), axis=0)
    sums = arrived[:, :, used].astype(f32) + arrived[:, :, used + 1].astype(f32)
    means = arrived[:, 0, used + 2].astype(f32)
    means = means[:, :PIX_ROWS] + means[:, HEAD_DIM : HEAD_DIM + PIX_ROWS]
    means = means - jnp.mean(means, axis=0, keepdims=True)
    correction = jnp.einsum("dr,dtc->trc", means, sums, precision=lax.Precision.HIGHEST)
    total = total + jnp.pad(correction, ((0, 0), (0, POS_ROWS), (0, 0)))
    piece = jnp.pad(total, ((0, 0), (0, ROWS - used), (0, 0))).astype(bf16)

    joined = jnp.zeros((3, PIECES, ROWS, group_cols), bf16)
    for k in range(PIECES):
        got = send(piece, lambda xc, yh, m, k=k: (m, yh ^ (k & 1), xc ^ (k >> 1)))
        slot = (mi ^ (k >> 1)) * 2 + (yhi ^ (k & 1))
        joined = lax.dynamic_update_slice(joined, got[:, None], (0, slot, 0, 0))
    joined = joined.reshape(3, PIECES * ROWS, group_cols)

    projected = jnp.einsum("ckp,tkn->tcpn", lhs, joined, preferred_element_type=f32)
    projected = projected.reshape(3, 8, patches, heads_here, HEAD_DIM)
    query = head_norm(projected[0], scale, query_gain).astype(bf16)
    key_vec = head_norm(projected[1], scale, key_gain).astype(bf16)
    value = (projected[2] * scale).astype(bf16)
    scores = jnp.einsum(
        "cphe,cshe->chps", query, key_vec, preferred_element_type=f32
    ) * HEAD_DIM ** (-0.5)
    exp_scores = jnp.exp(scores)
    probs = (exp_scores / jnp.sum(exp_scores, axis=-1, keepdims=True)).astype(bf16)
    head_out = jnp.einsum("chps,cshe->cphe", probs, value, preferred_element_type=f32)
    head_out = head_out.astype(bf16).reshape(8 * patches, group_cols)

    head_all = lax.all_gather(head_out, GROUP)
    attention = jnp.einsum("gtc,gcd->td", head_all, out_all, preferred_element_type=f32)
    output = embedded + attention.reshape(8, patches, 2 * cols)

    summed = (jnp.sum(output, axis=0) * (1.0 / 16)).reshape(patches, 2, cols)
    kept = lax.dynamic_index_in_dim(summed, yhi, 1, keepdims=True)
    sent = lax.dynamic_index_in_dim(summed, 1 - yhi, 1, keepdims=True)
    smoothed = kept + lax.ppermute(sent, "yh", [(0, 1), (1, 0)])

    moved = lax.all_to_all(output.astype(bf16), GROUP, 0, 0, tiled=True)
    moved = moved.reshape(4, 2, patches, 2, cols)
    features = jnp.transpose(moved, (2, 0, 3, 1, 4)).reshape(patches, 1, 1, width)
    return features, smoothed


def solution(mesh):
    fine = Mesh(mesh.devices.reshape(4, 2, 2, 2, 4), AXES)
    placed = (
        P(MP, None, None),
        P(MP, DP, None, None),
        P(None, DP),
        P(),
        P(),
        P(None, None, MP),
        P(),
        P(),
        P(MP, None),
    )
    return jax.shard_map(
        on_device,
        mesh=fine,
        in_specs=placed,
        out_specs=(P(None, DP, MP, None), P(None, MP, DP)),
        check_vma=False,
    )
```

```python
import jax
import jax.numpy as jnp
from jax import lax
from jax.experimental import pallas as pl
from jax.experimental.pallas import tpu as pltpu
from jax.sharding import Mesh
from jax.sharding import PartitionSpec as P

HEAD_DIM = 128
epsilon = 1e-06
bf16 = jnp.bfloat16
f32 = jnp.float32

AXES = ("x", "yh", "core", "yl", "z")
GROUP = ("x", "core")
DP = ("x", "yh", "core")
MP = ("yl", "z")
PIECES = 8
PIX_ROWS = 80
POS_ROWS = 16
ROWS = PIX_ROWS + POS_ROWS


def device_id(xc, yh, m):
    return (((xc // 2) * 2 + yh) * 2 + xc % 2) * 8 + m


def everyone():
    return [(xc, yh, m) for xc in range(8) for yh in range(2) for m in range(8)]


def send(array, target):
    pairs = [(device_id(*s), device_id(*target(*s))) for s in everyone()]
    return lax.ppermute(array, AXES, pairs)


def after(array, earlier):
    return lax.optimization_barrier((array, earlier))[0]


def pixel_pieces(rows):
    k, n = rows.shape
    return jnp.pad(rows, ((0, PIECES * PIX_ROWS - k), (0, 0))).reshape(PIECES, PIX_ROWS, n)


def extended(pixel_rows, pos_rows):
    n = pixel_rows.shape[1]
    both = [pixel_pieces(pixel_rows), pos_rows.reshape(PIECES, POS_ROWS, n)]
    return jnp.concatenate(both, axis=1).reshape(PIECES * ROWS, n)


def dot(left, right, dims):
    return lax.dot_general(left, right, (dims, ((), ())), preferred_element_type=f32)


def join_kernel(pixel_ref, pos_ref, gain_ref, qkv_ref, out_ref, mean_ref, acc_ref):
    step = pl.program_id(0)
    count = pl.num_programs(0)
    cols = gain_ref.shape[-1]

    @pl.when(step == 0)
    def _():
        total = jnp.zeros((PIX_ROWS, HEAD_DIM), f32)
        total_pos = jnp.zeros((POS_ROWS, HEAD_DIM), f32)
        for k in range(pixel_ref.shape[0]):
            for j in range(cols // HEAD_DIM):
                lanes = slice(j * HEAD_DIM, (j + 1) * HEAD_DIM)
                total += pixel_ref[k, :, lanes].astype(f32)
                total_pos += pos_ref[k, :, lanes].astype(f32)
        width = pixel_ref.shape[0] * cols
        mean_ref[:PIX_ROWS] = jnp.broadcast_to(
            jnp.sum(total, axis=1, keepdims=True) * (1.0 / width), (PIX_ROWS, HEAD_DIM)
        )
        mean_ref[PIX_ROWS:] = jnp.broadcast_to(
            jnp.sum(total_pos, axis=1, keepdims=True) * (1.0 / width), (POS_ROWS, HEAD_DIM)
        )
        acc_ref[...] = jnp.zeros_like(acc_ref)

    rows = jnp.concatenate([pixel_ref[step].astype(f32), pos_ref[step].astype(f32)], axis=0)
    centred = ((rows - mean_ref[:, :1]) * gain_ref[step]).astype(bf16)
    for t in range(3):
        acc_ref[t] += dot(centred, qkv_ref[t], ((1,), (0,)))

    @pl.when(step == count - 1)
    def _():
        group_cols = qkv_ref.shape[2]
        for t in range(3):
            out_ref[:, t * group_cols : (t + 1) * group_cols] = acc_ref[t].astype(bf16)


def join_weights(pixel_rows, pos_rows, gain, qkv):
    count, _, cols = pixel_rows.shape
    group_cols = qkv.shape[2]
    return pl.pallas_call(
        join_kernel,
        out_shape=jax.ShapeDtypeStruct((ROWS, 3 * group_cols), bf16),
        grid=(count,),
        in_specs=[
            pl.BlockSpec((count, PIX_ROWS, cols), lambda i: (0, 0, 0)),
            pl.BlockSpec((count, POS_ROWS, cols), lambda i: (0, 0, 0)),
            pl.BlockSpec((count, 1, cols), lambda i: (0, 0, 0)),
            pl.BlockSpec((3, cols, group_cols), lambda i: (0, i, 0)),
        ],
        out_specs=pl.BlockSpec((ROWS, 3 * group_cols), lambda i: (0, 0)),
        scratch_shapes=[
            pltpu.VMEM((ROWS, HEAD_DIM), f32),
            pltpu.VMEM((3, ROWS, group_cols), f32),
        ],
        cost_estimate=pl.CostEstimate(
            flops=6 * count * ROWS * cols * group_cols,
            transcendentals=0,
            bytes_accessed=6 * count * cols * group_cols,
        ),
        name="join_weights",
    )(pixel_rows, pos_rows, gain, qkv)


def head_norm(raw, scale, gain):
    average = jnp.mean(raw, axis=-1, keepdims=True)
    centred = raw - average
    variance = jnp.mean(centred * centred, axis=-1, keepdims=True)
    return (centred * (scale * lax.rsqrt(variance * scale * scale + epsilon)) * gain).astype(bf16)


def attention_kernel(lhs_ref, joined_ref, scale_ref, query_gain_ref, key_gain_ref, out_ref):
    projected = dot(lhs_ref[0], joined_ref[...], ((0,), (0,)))
    group_cols = projected.shape[1] // 3
    scale = scale_ref[0]
    for h in range(group_cols // HEAD_DIM):
        def part(t):
            start = t * group_cols + h * HEAD_DIM
            return projected[:, start : start + HEAD_DIM]

        query = head_norm(part(0), scale, query_gain_ref[...])
        key_vec = head_norm(part(1), scale, key_gain_ref[...])
        value = (part(2) * scale).astype(bf16)
        exp_scores = jnp.exp(dot(query, key_vec, ((1,), (1,))) * HEAD_DIM ** (-0.5))
        probs = (exp_scores / jnp.sum(exp_scores, axis=-1, keepdims=True)).astype(bf16)
        mixed = dot(probs, value, ((1,), (0,)))
        out_ref[0, :, h * HEAD_DIM : (h + 1) * HEAD_DIM] = mixed.astype(bf16)


def attend(lhs, joined, scale, query_gain, key_gain):
    copies, rows, patches = lhs.shape
    total_cols = joined.shape[1]
    return pl.pallas_call(
        attention_kernel,
        out_shape=jax.ShapeDtypeStruct((copies, patches, total_cols // 3), bf16),
        grid=(copies,),
        in_specs=[
            pl.BlockSpec((1, rows, patches), lambda i: (i, 0, 0)),
            pl.BlockSpec((rows, total_cols), lambda i: (0, 0)),
            pl.BlockSpec((1, patches, 1), lambda i: (i, 0, 0)),
            pl.BlockSpec((1, HEAD_DIM), lambda i: (0, 0)),
            pl.BlockSpec((1, HEAD_DIM), lambda i: (0, 0)),
        ],
        out_specs=pl.BlockSpec((1, patches, total_cols // 3), lambda i: (i, 0, 0)),
        cost_estimate=pl.CostEstimate(
            flops=4 * copies * rows * patches * total_cols,
            transcendentals=copies * patches * total_cols,
            bytes_accessed=40 * copies * patches * total_cols,
        ),
        name="attend",
    )(lhs, joined, scale, query_gain[None], key_gain[None])


def on_device(
    clean_image,
    noise_draw,
    embed_weight,
    position_table,
    norm_gain,
    qkv_weight,
    query_gain,
    key_gain,
    out_weight,
):
    xi, yhi, ci = (lax.axis_index(a) for a in ("x", "yh", "core"))
    patches, width = position_table.shape
    cols = embed_weight.shape[1]
    shares = width // cols

    def my_columns(array):
        start = (xi * 4 + ci) * cols
        return [
            lax.dynamic_slice_in_dim(array, start + yb * 2 * cols, cols, axis=1) for yb in range(2)
        ]

    mine = pixel_pieces(embed_weight).reshape(4, 1, 2, PIX_ROWS, cols)
    mine = jnp.broadcast_to(mine, (4, 2, 2, PIX_ROWS, cols)).reshape(shares, PIX_ROWS, cols)
    pixel_rows = lax.all_to_all(mine, DP, 0, 0, tiled=True)
    pos_rows = lax.dynamic_slice_in_dim(position_table, (2 * xi + ci) * POS_ROWS, POS_ROWS, axis=0)
    pos_rows = jnp.transpose(pos_rows.reshape(POS_ROWS, shares, cols), (1, 0, 2))
    piece = join_weights(
        pixel_rows,
        pos_rows,
        norm_gain.reshape(shares, 1, cols),
        jnp.transpose(qkv_weight, (1, 0, 2)),
    )
    piece = send(piece, lambda xc, yh, m: (m, yh, xc))
    joined = lax.all_gather(piece, MP, tiled=True)

    noisy = (clean_image[0].astype(f32) + 0.5 * noise_draw[0, 0].astype(f32)).astype(bf16)
    lhs_own = extended(noisy, jnp.eye(patches, dtype=bf16))
    lhs_own = after(lhs_own, mine)
    lhs = lax.all_to_all(jnp.broadcast_to(lhs_own[None], (8, *lhs_own.shape)), GROUP, 0, 0, tiled=True)

    other_weight = lax.ppermute(embed_weight, "yh", [(0, 1), (1, 0)])
    first = jnp.where(yhi == 0, embed_weight, other_weight)
    second = jnp.where(yhi == 0, other_weight, embed_weight)
    weight_two = extended(
        jnp.concatenate([first, second], axis=1),
        jnp.concatenate(my_columns(position_table), axis=1),
    )
    embedded = jnp.einsum("ckp,kd->cpd", lhs, weight_two, preferred_element_type=f32)

    average = jnp.mean(embedded, axis=-1)
    spread = jnp.mean(jnp.square(embedded - average[..., None]), axis=-1)
    stat = jnp.stack([average, spread])
    for bit in (1, 2, 4):
        other = send(stat, lambda xc, yh, m, bit=bit: (xc ^ bit, yh, m))
        gap = 0.5 * (stat[0] - other[0])
        stat = jnp.stack([0.5 * (stat[0] + other[0]), 0.5 * (stat[1] + other[1]) + gap * gap])
    scale = lax.rsqrt(stat[1] + epsilon)[..., None]

    out_mine = jnp.stack(my_columns(out_weight))
    out_mine = jnp.broadcast_to(out_mine[None], (8, *out_mine.shape))
    out_mine, joined = lax.optimization_barrier((out_mine, joined))
    out_all = lax.all_to_all(out_mine, MP, 0, 0, tiled=True)

    head_out = attend(lhs, joined, scale, query_gain, key_gain)
    head_out = head_out.reshape(8 * patches, -1)
    head_all = lax.all_gather(head_out, GROUP)
    halves = []
    for yb in range(2):
        attention = jnp.einsum("gtc,gcd->td", head_all, out_all[:, yb], preferred_element_type=f32)
        halves.append(
            embedded[:, :, yb * cols : (yb + 1) * cols] + attention.reshape(8, patches, cols)
        )
    output = jnp.stack(halves, axis=1)

    summed = jnp.sum(output, axis=0) * (1.0 / 16)
    kept = jnp.where(yhi == 0, summed[0], summed[1])
    sent = jnp.where(yhi == 0, summed[1], summed[0])
    smoothed = (kept + lax.ppermute(sent, "yh", [(0, 1), (1, 0)]))[:, None, :]

    moved = lax.all_to_all(output.astype(bf16), GROUP, 0, 0, tiled=True)
    blocks = [moved[2 * x + c, yb] for x in range(4) for yb in range(2) for c in range(2)]
    features = jnp.concatenate(blocks, axis=1).reshape(patches, 1, 1, width)
    return features, smoothed


def solution(mesh):
    fine = Mesh(mesh.devices.reshape(4, 2, 2, 2, 4), AXES)
    placed = (
        P(MP, None, None),
        P(MP, DP, None, None),
        P(None, DP),
        P(),
        P(),
        P(None, None, MP),
        P(),
        P(),
        P(MP, None),
    )
    return jax.shard_map(
        on_device,
        mesh=fine,
        in_specs=placed,
        out_specs=(P(None, DP, MP, None), P(None, MP, DP)),
        check_vma=False,
    )
```

```python
import jax
import jax.numpy as jnp
from jax import lax
from jax.experimental import pallas as pl
from jax.experimental.pallas import tpu as pltpu
from jax.sharding import Mesh
from jax.sharding import PartitionSpec as P


HEAD_DIM = 128
epsilon = 1e-06
bf16 = jnp.bfloat16
f32 = jnp.float32

AXES = ("x", "yh", "core", "yl", "z")
GROUP = ("x", "core")
DP = ("x", "yh", "core")
MP = ("yl", "z")
PIECES = 8
PIX_ROWS = 80
POS_ROWS = 16
ROWS = PIX_ROWS + POS_ROWS


def device_id(xc, yh, m):
    return (((xc // 2) * 2 + yh) * 2 + xc % 2) * 8 + m


def everyone():
    return [(xc, yh, m) for xc in range(8) for yh in range(2) for m in range(8)]


def send(array, target):
    pairs = [(device_id(*s), device_id(*target(*s))) for s in everyone()]
    return lax.ppermute(array, AXES, pairs)


def pixel_pieces(rows):
    k, n = rows.shape
    return jnp.pad(rows, ((0, PIECES * PIX_ROWS - k), (0, 0))).reshape(PIECES, PIX_ROWS, n)


def extended(pixel_rows, pos_rows):
    n = pixel_rows.shape[1]
    both = [pixel_pieces(pixel_rows), pos_rows.reshape(PIECES, POS_ROWS, n)]
    return jnp.concatenate(both, axis=1).reshape(PIECES * ROWS, n)


def dot(left, right, dims):
    return lax.dot_general(left, right, (dims, ((), ())), preferred_element_type=f32)


def join_kernel(piece_ref, pixel_ref, pos_all_ref, pos_ref, gain_ref, qkv_ref, out_ref, mean_ref, acc_ref):
    step = pl.program_id(0)
    shares, _, cols = pixel_ref.shape
    width = shares * cols

    @pl.when(step == 0)
    def _():
        total = jnp.zeros((PIX_ROWS, HEAD_DIM), f32)
        for k in range(shares):
            for j in range(cols // HEAD_DIM):
                total += pixel_ref[k, :, j * HEAD_DIM : (j + 1) * HEAD_DIM].astype(f32)
        total_pos = jnp.sum(pos_all_ref[...].astype(f32), axis=1, keepdims=True)
        total = jnp.sum(total, axis=1, keepdims=True)
        mean_ref[:PIX_ROWS] = jnp.broadcast_to(total * (1.0 / width), (PIX_ROWS, HEAD_DIM))
        mean_ref[PIX_ROWS:] = jnp.broadcast_to(total_pos * (1.0 / width), (POS_ROWS, HEAD_DIM))
        acc_ref[...] = jnp.zeros_like(acc_ref)

    per_step = qkv_ref.shape[1] // cols
    pixels = jnp.concatenate([pixel_ref[per_step * step + k] for k in range(per_step)], axis=1)
    rows = jnp.concatenate([pixels.astype(f32), pos_ref[...].astype(f32)], axis=0)
    centred = ((rows - mean_ref[:, :1]) * gain_ref[...]).astype(bf16)
    qkv = jnp.concatenate([qkv_ref[t] for t in range(3)], axis=1)
    acc_ref[...] += dot(centred, qkv, ((1,), (0,)))

    @pl.when(step == pl.num_programs(0) - 1)
    def _():
        out_ref[...] = acc_ref[...].astype(bf16)


def join_weights(piece, pixel_rows, position_table, gain, qkv):
    shares, _, cols = pixel_rows.shape
    width, group_cols = qkv.shape[1:]
    per_step = 2
    return pl.pallas_call(
        join_kernel,
        out_shape=jax.ShapeDtypeStruct((ROWS, 3 * group_cols), bf16),
        grid_spec=pltpu.PrefetchScalarGridSpec(
            num_scalar_prefetch=1,
            grid=(shares // per_step,),
            in_specs=[
                pl.BlockSpec((shares, PIX_ROWS, cols), lambda i, p: (0, 0, 0)),
                pl.BlockSpec((POS_ROWS, width), lambda i, p: (p[0], 0)),
                pl.BlockSpec((POS_ROWS, per_step * cols), lambda i, p: (p[0], i)),
                pl.BlockSpec((1, per_step * cols), lambda i, p: (0, i)),
                pl.BlockSpec((3, per_step * cols, group_cols), lambda i, p: (0, i, 0)),
            ],
            out_specs=pl.BlockSpec((ROWS, 3 * group_cols), lambda i, p: (0, 0)),
            scratch_shapes=[
                pltpu.VMEM((ROWS, HEAD_DIM), f32),
                pltpu.VMEM((ROWS, 3 * group_cols), f32),
            ],
        ),
        cost_estimate=pl.CostEstimate(
            flops=6 * width * ROWS * group_cols,
            transcendentals=0,
            bytes_accessed=6 * width * group_cols,
        ),
        name="join_weights",
    )(piece, pixel_rows, position_table, position_table, gain, qkv)


def head_norm(raw, scale, gain):
    average = jnp.mean(raw, axis=-1, keepdims=True)
    centred = raw - average
    variance = jnp.mean(centred * centred, axis=-1, keepdims=True)
    return (centred * (scale * lax.rsqrt(variance * scale * scale + epsilon)) * gain).astype(bf16)


def attention_kernel(
    lhs_ref, query_w_ref, key_w_ref, value_w_ref, scale_ref, query_gain_ref, key_gain_ref, out_ref, proj_ref
):
    copies, patches, rows = lhs_ref.shape
    weights = jnp.concatenate([query_w_ref[...], key_w_ref[...], value_w_ref[...]], axis=1)
    proj_ref[...] = dot(lhs_ref[...].reshape(copies * patches, rows), weights, ((1,), (0,)))
    diagonal = lax.broadcasted_iota(jnp.int32, (patches, patches), 0) == lax.broadcasted_iota(
        jnp.int32, (patches, patches), 1
    )
    for c in range(copies):
        here = slice(c * patches, (c + 1) * patches)
        scale_row = jnp.broadcast_to(scale_ref[c : c + 1, :], (patches, patches))
        scale = jnp.sum(jnp.where(diagonal, scale_row, 0.0), axis=1, keepdims=True)
        query = head_norm(proj_ref[here, :HEAD_DIM], scale, query_gain_ref[...])
        key_vec = head_norm(proj_ref[here, HEAD_DIM : 2 * HEAD_DIM], scale, key_gain_ref[...])
        value = (proj_ref[here, 2 * HEAD_DIM :] * scale).astype(bf16)
        exp_scores = jnp.exp(dot(query, key_vec, ((1,), (1,))) * HEAD_DIM ** (-0.5))
        probs = (exp_scores / jnp.sum(exp_scores, axis=-1, keepdims=True)).astype(bf16)
        out_ref[c] = dot(probs, value, ((1,), (0,))).astype(bf16)


def attend(lhs, joined, scale, query_gain, key_gain):
    copies, patches, rows = lhs.shape
    group_cols = joined.shape[1] // 3
    heads = group_cols // HEAD_DIM
    return pl.pallas_call(
        attention_kernel,
        out_shape=jax.ShapeDtypeStruct((copies, patches, group_cols), bf16),
        grid=(heads,),
        in_specs=[
            pl.BlockSpec((copies, patches, rows), lambda h: (0, 0, 0)),
            pl.BlockSpec((rows, HEAD_DIM), lambda h: (0, h)),
            pl.BlockSpec((rows, HEAD_DIM), lambda h: (0, heads + h)),
            pl.BlockSpec((rows, HEAD_DIM), lambda h: (0, 2 * heads + h)),
            pl.BlockSpec((copies, patches), lambda h: (0, 0)),
            pl.BlockSpec((1, HEAD_DIM), lambda h: (0, 0)),
            pl.BlockSpec((1, HEAD_DIM), lambda h: (0, 0)),
        ],
        out_specs=pl.BlockSpec((copies, patches, HEAD_DIM), lambda h: (0, 0, h)),
        scratch_shapes=[pltpu.VMEM((copies * patches, 3 * HEAD_DIM), f32)],
        cost_estimate=pl.CostEstimate(
            flops=4 * copies * rows * patches * group_cols * 3,
            transcendentals=copies * patches * group_cols,
            bytes_accessed=20 * copies * patches * group_cols,
        ),
        name="attend",
    )(lhs, joined, joined, joined, scale, query_gain[None], key_gain[None])


def assemble_kernel(in_ref, out_ref):
    cores, halves, _, cols = in_ref.shape
    for yb in range(halves):
        for c in range(cores):
            start = (yb * cores + c) * cols
            out_ref[:, start : start + cols] = in_ref[c, yb]


def assemble(moved):
    shares, halves, patches, cols = moved.shape
    return pl.pallas_call(
        assemble_kernel,
        out_shape=jax.ShapeDtypeStruct((patches, shares * halves * cols), bf16),
        grid=(shares // 2,),
        in_specs=[pl.BlockSpec((2, halves, patches, cols), lambda i: (i, 0, 0, 0))],
        out_specs=pl.BlockSpec((patches, 2 * halves * cols), lambda i: (0, i)),
        name="assemble",
    )(moved)


def block(
    clean_image,
    noise_draw,
    embed_weight,
    position_table,
    norm_gain,
    qkv_weight,
    query_gain,
    key_gain,
    out_weight,
):
    xi, yhi, ci = (lax.axis_index(a) for a in ("x", "yh", "core"))
    patches, width = position_table.shape
    cols = embed_weight.shape[1]
    shares = width // cols

    def my_columns(array):
        start = (xi * 4 + ci) * cols
        return [
            lax.dynamic_slice_in_dim(array, start + yb * 2 * cols, cols, axis=1) for yb in range(2)
        ]

    noisy = (clean_image[0].astype(f32) + 0.5 * noise_draw[0, 0].astype(f32)).astype(bf16)
    lhs_own = extended(noisy, jnp.eye(patches, dtype=bf16)).T
    lhs = lax.all_gather(lhs_own, GROUP)

    mine = pixel_pieces(embed_weight).reshape(4, 1, 2, PIX_ROWS, cols)
    mine = jnp.broadcast_to(mine, (4, 2, 2, PIX_ROWS, cols)).reshape(shares, PIX_ROWS, cols)
    pixel_rows = lax.all_to_all(mine, DP, 0, 0, tiled=True)
    out_mine = jnp.stack(my_columns(out_weight))
    out_mine = jnp.broadcast_to(out_mine[None], (8, *out_mine.shape))
    out_mine, pixel_rows, own_weight = lax.optimization_barrier((out_mine, pixel_rows, embed_weight))
    piece = join_weights(
        (2 * xi + ci).astype(jnp.int32).reshape(1),
        pixel_rows,
        position_table,
        norm_gain[None],
        jnp.transpose(qkv_weight, (1, 0, 2)),
    )
    piece = send(piece, lambda xc, yh, m: (m, yh, xc))
    joined = jnp.broadcast_to(piece[None], (8, *piece.shape))
    joined = lax.all_to_all(joined, MP, 0, 0, tiled=True).reshape(8 * ROWS, -1)

    other_weight = lax.ppermute(own_weight, "yh", [(0, 1), (1, 0)])
    first = jnp.where(yhi == 0, embed_weight, other_weight)
    second = jnp.where(yhi == 0, other_weight, embed_weight)
    weight_two = extended(
        jnp.concatenate([first, second], axis=1),
        jnp.concatenate(my_columns(position_table), axis=1),
    )
    embedded = jnp.einsum("cpk,kd->cpd", lhs, weight_two, preferred_element_type=f32)

    average = jnp.mean(embedded, axis=-1)
    spread = jnp.mean(jnp.square(embedded - average[..., None]), axis=-1)
    stat = jnp.stack([average, spread])
    stats = [stat]
    for k in range(1, 8):
        stats.append(send(stat, lambda xc, yh, m, k=k: (xc ^ k, yh, m)))
    average = sum(each[0] for each in stats) * 0.125
    spread = sum(each[1] + jnp.square(each[0] - average) for each in stats) * 0.125
    scale = lax.rsqrt(spread + epsilon)

    out_mine, joined = lax.optimization_barrier((out_mine, joined))
    out_all = lax.all_to_all(out_mine, MP, 0, 0, tiled=True)

    head_out = attend(lhs, joined, scale, query_gain, key_gain)
    head_out = head_out.reshape(8 * patches, -1)
    head_all = lax.all_gather(head_out, GROUP)
    halves = []
    for yb in range(2):
        attention = jnp.einsum("gtc,gcd->td", head_all, out_all[:, yb], preferred_element_type=f32)
        halves.append(
            embedded[:, :, yb * cols : (yb + 1) * cols] + attention.reshape(8, patches, cols)
        )
    output = jnp.stack(halves, axis=1)

    summed = jnp.sum(output, axis=0) * (1.0 / 16)
    kept = jnp.where(yhi == 0, summed[0], summed[1])
    sent = jnp.where(yhi == 0, summed[1], summed[0])
    smoothed = (kept + lax.ppermute(sent, "yh", [(0, 1), (1, 0)]))[:, None, :]

    moved = lax.all_to_all(output.astype(bf16), GROUP, 0, 0, tiled=True)
    features = assemble(moved).reshape(patches, 1, 1, width)
    return features, smoothed


def solution(mesh):
    fine = Mesh(mesh.devices.reshape(4, 2, 2, 2, 4), AXES)
    placed = (
        P(MP, None, None),
        P(MP, DP, None, None),
        P(None, DP),
        P(),
        P(),
        P(None, None, MP),
        P(),
        P(),
        P(MP, None),
    )
    return jax.shard_map(
        block,
        mesh=fine,
        in_specs=placed,
        out_specs=(P(None, DP, MP, None), P(None, MP, DP)),
        check_vma=False,
    )
```

```python
import jax
import jax.numpy as jnp
from jax import lax
from jax.experimental import pallas as pl
from jax.experimental.pallas import tpu as pltpu
from jax.sharding import Mesh
from jax.sharding import PartitionSpec as P


HEAD_DIM = 128
epsilon = 1e-06
bf16 = jnp.bfloat16
f32 = jnp.float32

AXES = ("x", "yh", "core", "yl", "z")
GROUP = ("x", "core")
DP = ("x", "yh", "core")
MP = ("yl", "z")
PIECES = 8
PIX_ROWS = 80
POS_ROWS = 16
ROWS = PIX_ROWS + POS_ROWS


def device_id(xc, yh, m):
    return (((xc // 2) * 2 + yh) * 2 + xc % 2) * 8 + m


def everyone():
    return [(xc, yh, m) for xc in range(8) for yh in range(2) for m in range(8)]


def send(array, target):
    pairs = [(device_id(*s), device_id(*target(*s))) for s in everyone()]
    return lax.ppermute(array, AXES, pairs)


def pixel_pieces(rows):
    k, n = rows.shape
    return jnp.pad(rows, ((0, PIECES * PIX_ROWS - k), (0, 0))).reshape(PIECES, PIX_ROWS, n)


def extended(pixel_rows, pos_rows):
    n = pixel_rows.shape[1]
    both = [pixel_pieces(pixel_rows), pos_rows.reshape(PIECES, POS_ROWS, n)]
    return jnp.concatenate(both, axis=1).reshape(PIECES * ROWS, n)


def dot(left, right, dims):
    return lax.dot_general(left, right, (dims, ((), ())), preferred_element_type=f32)


def join_kernel(piece_ref, pixel_ref, pos_all_ref, pos_ref, gain_ref, qkv_ref, out_ref, mean_ref, acc_ref):
    step = pl.program_id(0)
    shares, _, cols = pixel_ref.shape
    width = shares * cols

    @pl.when(step == 0)
    def _():
        total = jnp.zeros((PIX_ROWS, HEAD_DIM), f32)
        for k in range(shares):
            for j in range(cols // HEAD_DIM):
                total += pixel_ref[k, :, j * HEAD_DIM : (j + 1) * HEAD_DIM].astype(f32)
        total_pos = jnp.sum(pos_all_ref[...].astype(f32), axis=1, keepdims=True)
        total = jnp.sum(total, axis=1, keepdims=True)
        mean_ref[:PIX_ROWS] = jnp.broadcast_to(total * (1.0 / width), (PIX_ROWS, HEAD_DIM))
        mean_ref[PIX_ROWS:] = jnp.broadcast_to(total_pos * (1.0 / width), (POS_ROWS, HEAD_DIM))
        acc_ref[...] = jnp.zeros_like(acc_ref)

    per_step = qkv_ref.shape[1] // cols
    pixels = jnp.concatenate([pixel_ref[per_step * step + k] for k in range(per_step)], axis=1)
    rows = jnp.concatenate([pixels.astype(f32), pos_ref[...].astype(f32)], axis=0)
    centred = ((rows - mean_ref[:, :1]) * gain_ref[...]).astype(bf16)
    qkv = jnp.concatenate([qkv_ref[t] for t in range(3)], axis=1)
    acc_ref[...] += dot(centred, qkv, ((1,), (0,)))

    @pl.when(step == pl.num_programs(0) - 1)
    def _():
        for j in range(acc_ref.shape[1] // HEAD_DIM):
            lanes = slice(j * HEAD_DIM, (j + 1) * HEAD_DIM)
            block = acc_ref[:, lanes]
            if 3 * j < 2 * (acc_ref.shape[1] // HEAD_DIM):
                block = block - jnp.mean(block, axis=1, keepdims=True)
            out_ref[:, lanes] = block.astype(bf16)


def join_weights(piece, pixel_rows, position_table, gain, qkv):
    shares, _, cols = pixel_rows.shape
    width, group_cols = qkv.shape[1:]
    per_step = 2
    return pl.pallas_call(
        join_kernel,
        out_shape=jax.ShapeDtypeStruct((ROWS, 3 * group_cols), bf16),
        grid_spec=pltpu.PrefetchScalarGridSpec(
            num_scalar_prefetch=1,
            grid=(shares // per_step,),
            in_specs=[
                pl.BlockSpec((shares, PIX_ROWS, cols), lambda i, p: (0, 0, 0)),
                pl.BlockSpec((POS_ROWS, width), lambda i, p: (p[0], 0)),
                pl.BlockSpec((POS_ROWS, per_step * cols), lambda i, p: (p[0], i)),
                pl.BlockSpec((1, per_step * cols), lambda i, p: (0, i)),
                pl.BlockSpec((3, per_step * cols, group_cols), lambda i, p: (0, i, 0)),
            ],
            out_specs=pl.BlockSpec((ROWS, 3 * group_cols), lambda i, p: (0, 0)),
            scratch_shapes=[
                pltpu.VMEM((ROWS, HEAD_DIM), f32),
                pltpu.VMEM((ROWS, 3 * group_cols), f32),
            ],
        ),
        cost_estimate=pl.CostEstimate(
            flops=6 * width * ROWS * group_cols,
            transcendentals=0,
            bytes_accessed=6 * width * group_cols,
        ),
        name="join_weights",
    )(piece, pixel_rows, position_table, position_table, gain, qkv)


def head_norm(centred, scale, gain):
    variance = jnp.mean(centred * centred, axis=-1, keepdims=True)
    return (centred * (scale * lax.rsqrt(variance * (scale * scale) + epsilon)) * gain).astype(bf16)


def attention_kernel(
    lhs_ref, query_w_ref, key_w_ref, value_w_ref, scale_ref, query_gain_ref, key_gain_ref, out_ref, proj_ref, scale_all
):
    copies, patches, rows = lhs_ref.shape

    @pl.when(pl.program_id(0) == 0)
    def _():
        shape = (patches, patches)
        diagonal = lax.broadcasted_iota(jnp.int32, shape, 0) == lax.broadcasted_iota(jnp.int32, shape, 1)
        for c in range(copies):
            row = jnp.broadcast_to(scale_ref[c : c + 1, :], shape)
            column = jnp.sum(jnp.where(diagonal, row, 0.0), axis=1, keepdims=True)
            scale_all[c] = jnp.broadcast_to(column, (patches, HEAD_DIM))

    weights = jnp.concatenate([query_w_ref[...], key_w_ref[...], value_w_ref[...]], axis=1)
    proj_ref[...] = dot(lhs_ref[...].reshape(copies * patches, rows), weights, ((1,), (0,)))
    ones = jnp.ones((patches, HEAD_DIM), bf16)
    for c in range(copies):
        here = slice(c * patches, (c + 1) * patches)
        scale = scale_all[c]
        query = head_norm(proj_ref[here, :HEAD_DIM], scale, query_gain_ref[...])
        key_vec = head_norm(proj_ref[here, HEAD_DIM : 2 * HEAD_DIM], scale, key_gain_ref[...])
        value = (proj_ref[here, 2 * HEAD_DIM :] * scale).astype(bf16)
        exp_scores = jnp.exp(dot(query, key_vec, ((1,), (1,))) * HEAD_DIM ** (-0.5)).astype(bf16)
        mixed = dot(exp_scores, jnp.concatenate([value, ones], axis=1), ((1,), (0,)))
        out_ref[c] = (mixed[:, :HEAD_DIM] / mixed[:, HEAD_DIM:]).astype(bf16)


def attend(lhs, joined, scale, query_gain, key_gain):
    copies, patches, rows = lhs.shape
    group_cols = joined.shape[1] // 3
    heads = group_cols // HEAD_DIM
    return pl.pallas_call(
        attention_kernel,
        out_shape=jax.ShapeDtypeStruct((copies, patches, group_cols), bf16),
        grid=(heads,),
        in_specs=[
            pl.BlockSpec((copies, patches, rows), lambda h: (0, 0, 0)),
            pl.BlockSpec((rows, HEAD_DIM), lambda h: (0, h)),
            pl.BlockSpec((rows, HEAD_DIM), lambda h: (0, heads + h)),
            pl.BlockSpec((rows, HEAD_DIM), lambda h: (0, 2 * heads + h)),
            pl.BlockSpec((copies, patches), lambda h: (0, 0)),
            pl.BlockSpec((1, HEAD_DIM), lambda h: (0, 0)),
            pl.BlockSpec((1, HEAD_DIM), lambda h: (0, 0)),
        ],
        out_specs=pl.BlockSpec((copies, patches, HEAD_DIM), lambda h: (0, 0, h)),
        scratch_shapes=[
            pltpu.VMEM((copies * patches, 3 * HEAD_DIM), f32),
            pltpu.VMEM((copies, patches, HEAD_DIM), f32),
        ],
        cost_estimate=pl.CostEstimate(
            flops=4 * copies * rows * patches * group_cols * 3,
            transcendentals=copies * patches * group_cols,
            bytes_accessed=20 * copies * patches * group_cols,
        ),
        name="attend",
    )(lhs, joined, joined, joined, scale, query_gain[None], key_gain[None])


def assemble_kernel(in_ref, out_ref, sems):
    shares, _, both = in_ref.shape
    cols = both // 2
    copies = []
    for g in range(shares):
        for yb in range(2):
            start = ((g // 2 * 2 + yb) * 2 + g % 2) * cols
            copies.append(
                pltpu.make_async_copy(
                    in_ref.at[g, :, yb * cols : (yb + 1) * cols],
                    out_ref.at[:, start : start + cols],
                    sems.at[g, yb],
                )
            )
    for copy in copies:
        copy.start()
    for copy in copies:
        copy.wait()


def assemble(moved):
    shares, patches, both = moved.shape
    return pl.pallas_call(
        assemble_kernel,
        out_shape=jax.ShapeDtypeStruct((patches, shares * both), bf16),
        in_specs=[pl.BlockSpec(memory_space=pl.ANY)],
        out_specs=pl.BlockSpec(memory_space=pl.ANY),
        scratch_shapes=[pltpu.SemaphoreType.DMA((shares, 2))],
        name="assemble",
    )(moved)


def block(
    clean_image,
    noise_draw,
    embed_weight,
    position_table,
    norm_gain,
    qkv_weight,
    query_gain,
    key_gain,
    out_weight,
):
    xi, yhi, ci = (lax.axis_index(a) for a in ("x", "yh", "core"))
    patches, width = position_table.shape
    cols = embed_weight.shape[1]
    shares = width // cols

    def my_columns(array):
        start = (xi * 4 + ci) * cols
        return [
            lax.dynamic_slice_in_dim(array, start + yb * 2 * cols, cols, axis=1) for yb in range(2)
        ]

    mine = pixel_pieces(embed_weight).reshape(4, 1, 2, PIX_ROWS, cols)
    mine = jnp.broadcast_to(mine, (4, 2, 2, PIX_ROWS, cols)).reshape(shares, PIX_ROWS, cols)
    pixel_rows = lax.all_to_all(mine, DP, 0, 0, tiled=True)
    noisy = (clean_image[0].astype(f32) + 0.5 * noise_draw[0, 0].astype(f32)).astype(bf16)
    lhs_own = extended(noisy, jnp.eye(patches, dtype=bf16)).T
    out_mine = jnp.concatenate(my_columns(out_weight), axis=1)
    out_mine = jnp.broadcast_to(out_mine[None], (8, *out_mine.shape))
    out_mine, lhs_own, pixel_rows, own_weight = lax.optimization_barrier(
        (out_mine, lhs_own, pixel_rows, embed_weight)
    )
    lhs = lax.all_gather(lhs_own, GROUP)
    piece = join_weights(
        (2 * xi + ci).astype(jnp.int32).reshape(1),
        pixel_rows,
        position_table,
        norm_gain[None],
        jnp.transpose(qkv_weight, (1, 0, 2)),
    )
    piece = send(piece, lambda xc, yh, m: (m, yh, xc))
    joined = jnp.broadcast_to(piece[None], (8, *piece.shape))
    joined = lax.all_to_all(joined, MP, 0, 0, tiled=True).reshape(8 * ROWS, -1)

    other_weight = lax.ppermute(own_weight, "yh", [(0, 1), (1, 0)])
    first = jnp.where(yhi == 0, embed_weight, other_weight)
    second = jnp.where(yhi == 0, other_weight, embed_weight)
    weight_two = extended(
        jnp.concatenate([first, second], axis=1),
        jnp.concatenate(my_columns(position_table), axis=1),
    )
    embedded = jnp.einsum("cpk,kd->cpd", lhs, weight_two, preferred_element_type=f32)

    average = jnp.mean(embedded, axis=-1)
    spread = jnp.mean(jnp.square(embedded - average[..., None]), axis=-1)
    stat = jnp.stack([average, spread])
    stats = [stat]
    for k in range(1, 8):
        stats.append(send(stat, lambda xc, yh, m, k=k: (xc ^ k, yh, m)))
    average = sum(each[0] for each in stats) * 0.125
    spread = sum(each[1] + jnp.square(each[0] - average) for each in stats) * 0.125
    scale = lax.rsqrt(spread + epsilon)

    out_mine, joined = lax.optimization_barrier((out_mine, joined))
    out_all = lax.all_to_all(out_mine, MP, 0, 0, tiled=True)

    head_out = attend(lhs, joined, scale, query_gain, key_gain)
    head_out = head_out.reshape(8 * patches, -1)
    head_all = lax.all_gather(head_out, GROUP)
    attention = jnp.einsum("gtc,gcd->td", head_all, out_all, preferred_element_type=f32)
    output = embedded + attention.reshape(8, patches, 2 * cols)

    summed = jnp.sum(output, axis=0) * (1.0 / 16)
    kept = jnp.where(yhi == 0, summed[:, :cols], summed[:, cols:])
    sent = jnp.where(yhi == 0, summed[:, cols:], summed[:, :cols])
    smoothed = (kept + lax.ppermute(sent, "yh", [(0, 1), (1, 0)]))[:, None, :]

    moved = lax.all_to_all(output.astype(bf16), GROUP, 0, 0, tiled=True)
    features = assemble(moved).reshape(patches, 1, 1, width)
    return features, smoothed


def solution(mesh):
    fine = Mesh(mesh.devices.reshape(4, 2, 2, 2, 4), AXES)
    placed = (
        P(MP, None, None),
        P(MP, DP, None, None),
        P(None, DP),
        P(),
        P(),
        P(None, None, MP),
        P(),
        P(),
        P(MP, None),
    )
    return jax.shard_map(
        block,
        mesh=fine,
        in_specs=placed,
        out_specs=(P(None, DP, MP, None), P(None, MP, DP)),
        check_vma=False,
    )
```

```python
import jax
import jax.numpy as jnp
from jax import lax
from jax.experimental import pallas as pl
from jax.experimental.pallas import tpu as pltpu
from jax.sharding import Mesh
from jax.sharding import PartitionSpec as P


HEAD_DIM = 128
epsilon = 1e-06
bf16 = jnp.bfloat16
f32 = jnp.float32

AXES = ("x", "yh", "core", "yl", "z")
GROUP = ("x", "core")
DP = ("x", "yh", "core")
MP = ("yl", "z")
PIECES = 8
PIX_ROWS = 80
POS_ROWS = 16
ROWS = PIX_ROWS + POS_ROWS


def device_id(xc, yh, m):
    return (((xc // 2) * 2 + yh) * 2 + xc % 2) * 8 + m


def everyone():
    return [(xc, yh, m) for xc in range(8) for yh in range(2) for m in range(8)]


NEAR = [
    [device_id(2 * x + c, yh, ((yh ^ s) * 4 + z)) for x in range(4) for yh in range(2) for c in range(2)]
    for s in range(2)
    for z in range(4)
]


def send(array, target):
    pairs = [(device_id(*s), device_id(*target(*s))) for s in everyone()]
    return lax.ppermute(array, AXES, pairs)


def pixel_pieces(rows):
    k, n = rows.shape
    return jnp.pad(rows, ((0, PIECES * PIX_ROWS - k), (0, 0))).reshape(PIECES, PIX_ROWS, n)


def dot(left, right, dims):
    return lax.dot_general(left, right, (dims, ((), ())), preferred_element_type=f32)


def join_kernel(piece_ref, pixel_ref, pos_all_ref, pos_ref, gain_ref, qkv_ref, out_ref, mean_ref, acc_ref):
    step = pl.program_id(0)
    shares, _, cols = pixel_ref.shape
    width = shares * cols

    @pl.when(step == 0)
    def _():
        total = jnp.zeros((PIX_ROWS, HEAD_DIM), f32)
        for k in range(shares):
            for j in range(cols // HEAD_DIM):
                total += pixel_ref[k, :, j * HEAD_DIM : (j + 1) * HEAD_DIM].astype(f32)
        total_pos = jnp.sum(pos_all_ref[...].astype(f32), axis=1, keepdims=True)
        total = jnp.sum(total, axis=1, keepdims=True)
        mean_ref[:PIX_ROWS] = jnp.broadcast_to(total * (1.0 / width), (PIX_ROWS, HEAD_DIM))
        mean_ref[PIX_ROWS:] = jnp.broadcast_to(total_pos * (1.0 / width), (POS_ROWS, HEAD_DIM))
        acc_ref[...] = jnp.zeros_like(acc_ref)

    per_step = qkv_ref.shape[1] // cols
    pixels = jnp.concatenate([pixel_ref[per_step * step + k] for k in range(per_step)], axis=1)
    rows = jnp.concatenate([pixels.astype(f32), pos_ref[...].astype(f32)], axis=0)
    centred = ((rows - mean_ref[:, :1]) * gain_ref[...]).astype(bf16)
    qkv = jnp.concatenate([qkv_ref[t] for t in range(3)], axis=1)
    acc_ref[...] += dot(centred, qkv, ((1,), (0,)))

    @pl.when(step == pl.num_programs(0) - 1)
    def _():
        for j in range(acc_ref.shape[1] // HEAD_DIM):
            lanes = slice(j * HEAD_DIM, (j + 1) * HEAD_DIM)
            block = acc_ref[:, lanes]
            if 3 * j < 2 * (acc_ref.shape[1] // HEAD_DIM):
                block = block - jnp.mean(block, axis=1, keepdims=True)
            out_ref[:, lanes] = block.astype(bf16)


def join_weights(piece, pixel_rows, position_table, gain, qkv):
    shares, _, cols = pixel_rows.shape
    width, group_cols = qkv.shape[1:]
    per_step = 2
    return pl.pallas_call(
        join_kernel,
        out_shape=jax.ShapeDtypeStruct((ROWS, 3 * group_cols), bf16),
        grid_spec=pltpu.PrefetchScalarGridSpec(
            num_scalar_prefetch=1,
            grid=(shares // per_step,),
            in_specs=[
                pl.BlockSpec((shares, PIX_ROWS, cols), lambda i, p: (0, 0, 0)),
                pl.BlockSpec((POS_ROWS, width), lambda i, p: (p[0], 0)),
                pl.BlockSpec((POS_ROWS, per_step * cols), lambda i, p: (p[0], i)),
                pl.BlockSpec((1, per_step * cols), lambda i, p: (0, i)),
                pl.BlockSpec((3, per_step * cols, group_cols), lambda i, p: (0, i, 0)),
            ],
            out_specs=pl.BlockSpec((ROWS, 3 * group_cols), lambda i, p: (0, 0)),
            scratch_shapes=[
                pltpu.VMEM((ROWS, HEAD_DIM), f32),
                pltpu.VMEM((ROWS, 3 * group_cols), f32),
            ],
        ),
        cost_estimate=pl.CostEstimate(
            flops=6 * width * ROWS * group_cols,
            transcendentals=0,
            bytes_accessed=6 * width * group_cols,
        ),
        name="join_weights",
    )(piece, pixel_rows, position_table, position_table, gain, qkv)


def head_norm(centred, scale, gain):
    variance = jnp.mean(centred * centred, axis=-1, keepdims=True)
    return (centred * (scale * lax.rsqrt(variance * (scale * scale) + epsilon)) * gain).astype(bf16)


def attention_kernel(
    lhs_ref, query_w_ref, key_w_ref, value_w_ref, query_p_ref, key_p_ref, value_p_ref,
    scale_ref, query_gain_ref, key_gain_ref, out_ref, proj_ref, scale_all,
):
    copies, patches, rows = lhs_ref.shape

    @pl.when(pl.program_id(0) == 0)
    def _():
        shape = (patches, patches)
        diagonal = lax.broadcasted_iota(jnp.int32, shape, 0) == lax.broadcasted_iota(jnp.int32, shape, 1)
        for c in range(copies):
            row = jnp.broadcast_to(scale_ref[c : c + 1, :], shape)
            column = jnp.sum(jnp.where(diagonal, row, 0.0), axis=1, keepdims=True)
            scale_all[c] = jnp.broadcast_to(column, (patches, HEAD_DIM))

    weights = jnp.concatenate([query_w_ref[...], key_w_ref[...], value_w_ref[...]], axis=2)
    weights = weights.reshape(rows, 3 * HEAD_DIM)
    proj_ref[...] = dot(lhs_ref[...].reshape(copies * patches, rows), weights, ((1,), (0,)))
    query_p, key_p, value_p = (
        ref[...].astype(f32).reshape(patches, HEAD_DIM) for ref in (query_p_ref, key_p_ref, value_p_ref)
    )
    ones = jnp.ones((patches, HEAD_DIM), bf16)
    for c in range(copies):
        here = slice(c * patches, (c + 1) * patches)
        scale = scale_all[c]
        query = head_norm(proj_ref[here, :HEAD_DIM] + query_p, scale, query_gain_ref[...])
        key_vec = head_norm(proj_ref[here, HEAD_DIM : 2 * HEAD_DIM] + key_p, scale, key_gain_ref[...])
        value = ((proj_ref[here, 2 * HEAD_DIM :] + value_p) * scale).astype(bf16)
        exp_scores = jnp.exp(dot(query, key_vec, ((1,), (1,))) * HEAD_DIM ** (-0.5)).astype(bf16)
        mixed = dot(exp_scores, jnp.concatenate([value, ones], axis=1), ((1,), (0,)))
        out_ref[c] = (mixed[:, :HEAD_DIM] / mixed[:, HEAD_DIM:]).astype(bf16)


def attend(lhs, joined, scale, query_gain, key_gain):
    copies, patches, rows = lhs.shape
    group_cols = joined.shape[2] // 3
    heads = group_cols // HEAD_DIM

    def columns(t, count, first):
        return pl.BlockSpec((PIECES, count, HEAD_DIM), lambda h: (0, first // count, t * heads + h))

    return pl.pallas_call(
        attention_kernel,
        out_shape=jax.ShapeDtypeStruct((copies, patches, group_cols), bf16),
        grid=(heads,),
        in_specs=[
            pl.BlockSpec((copies, patches, rows), lambda h: (0, 0, 0)),
            *[columns(t, PIX_ROWS, 0) for t in range(3)],
            *[columns(t, POS_ROWS, PIX_ROWS) for t in range(3)],
            pl.BlockSpec((copies, patches), lambda h: (0, 0)),
            pl.BlockSpec((1, HEAD_DIM), lambda h: (0, 0)),
            pl.BlockSpec((1, HEAD_DIM), lambda h: (0, 0)),
        ],
        out_specs=pl.BlockSpec((copies, patches, HEAD_DIM), lambda h: (0, 0, h)),
        scratch_shapes=[
            pltpu.VMEM((copies * patches, 3 * HEAD_DIM), f32),
            pltpu.VMEM((copies, patches, HEAD_DIM), f32),
        ],
        cost_estimate=pl.CostEstimate(
            flops=4 * copies * rows * patches * group_cols * 3,
            transcendentals=copies * patches * group_cols,
            bytes_accessed=20 * copies * patches * group_cols,
        ),
        name="attend",
    )(lhs, *[joined] * 6, scale, query_gain[None], key_gain[None])


def assemble_kernel(in_ref, out_ref):
    cores, _, both = in_ref.shape
    cols = both // 2
    for yb in range(2):
        for c in range(cores):
            start = (yb * cores + c) * cols
            out_ref[:, start : start + cols] = in_ref[c, :, yb * cols : (yb + 1) * cols]


def assemble(moved):
    shares, patches, both = moved.shape
    return pl.pallas_call(
        assemble_kernel,
        out_shape=jax.ShapeDtypeStruct((patches, shares * both), bf16),
        grid=(shares // 2,),
        in_specs=[pl.BlockSpec((2, patches, both), lambda i: (i, 0, 0))],
        out_specs=pl.BlockSpec((patches, 2 * both), lambda i: (0, i)),
        name="assemble",
    )(moved)


def block(
    clean_image,
    noise_draw,
    embed_weight,
    position_table,
    norm_gain,
    qkv_weight,
    query_gain,
    key_gain,
    out_weight,
):
    xi, yhi, ci = (lax.axis_index(a) for a in ("x", "yh", "core"))
    patches, width = position_table.shape
    cols = embed_weight.shape[1]
    shares = width // cols

    def my_columns(array):
        start = (xi * 4 + ci) * cols
        return [
            lax.dynamic_slice_in_dim(array, start + yb * 2 * cols, cols, axis=1) for yb in range(2)
        ]

    mine = pixel_pieces(embed_weight).reshape(4, 1, 2, PIX_ROWS, cols)
    mine = jnp.broadcast_to(mine, (4, 2, 2, PIX_ROWS, cols)).reshape(shares, PIX_ROWS, cols)
    pixel_rows = lax.all_to_all(mine, AXES, 0, 0, axis_index_groups=NEAR, tiled=True)
    noisy = (clean_image[0].astype(f32) + 0.5 * noise_draw[0, 0].astype(f32)).astype(bf16)
    lhs_own = jnp.pad(noisy, ((0, PIECES * PIX_ROWS - noisy.shape[0]), (0, 0))).T
    out_mine = jnp.concatenate(my_columns(out_weight), axis=1)
    out_mine = jnp.broadcast_to(out_mine[None], (8, *out_mine.shape))
    out_mine, lhs_own, pixel_rows, own_weight = lax.optimization_barrier(
        (out_mine, lhs_own, pixel_rows, embed_weight)
    )
    lhs = lax.all_gather(lhs_own, GROUP)
    piece = join_weights(
        (2 * xi + ci).astype(jnp.int32).reshape(1),
        pixel_rows,
        position_table,
        norm_gain[None],
        jnp.transpose(qkv_weight, (1, 0, 2)),
    )
    piece = send(piece, lambda xc, yh, m: (m, yh, xc))
    joined = jnp.broadcast_to(piece[None], (8, *piece.shape))
    joined = lax.all_to_all(joined, MP, 0, 0, tiled=True)

    other_weight = send(own_weight, lambda xc, yh, m: (xc, 1 - yh, m ^ 4))
    first = jnp.where(yhi == 0, embed_weight, other_weight)
    second = jnp.where(yhi == 0, other_weight, embed_weight)
    weight_two = jnp.concatenate([first, second], axis=1)
    weight_two = jnp.pad(weight_two, ((0, PIECES * PIX_ROWS - weight_two.shape[0]), (0, 0)))
    position_two = jnp.concatenate(my_columns(position_table), axis=1).astype(f32)
    embedded = jnp.einsum("cpk,kd->cpd", lhs, weight_two, preferred_element_type=f32) + position_two

    average = jnp.mean(embedded, axis=-1)
    spread = jnp.mean(jnp.square(embedded - average[..., None]), axis=-1)
    stat = jnp.stack([average, spread])
    stats = [stat]
    for k in range(1, 8):
        stats.append(send(stat, lambda xc, yh, m, k=k: (xc ^ k, yh, m)))
    average = sum(each[0] for each in stats) * 0.125
    spread = sum(each[1] + jnp.square(each[0] - average) for each in stats) * 0.125
    scale = lax.rsqrt(spread + epsilon)

    out_mine, joined = lax.optimization_barrier((out_mine, joined))
    out_all = lax.all_to_all(out_mine, MP, 0, 0, tiled=True)

    head_out = attend(lhs, joined, scale, query_gain, key_gain)
    head_out = head_out.reshape(8 * patches, -1)
    head_all = lax.all_gather(head_out, GROUP)
    attention = jnp.einsum("gtc,gcd->td", head_all, out_all, preferred_element_type=f32)
    output = embedded + attention.reshape(8, patches, 2 * cols)

    summed = jnp.sum(output, axis=0) * (1.0 / 16)
    kept = jnp.where(yhi == 0, summed[:, :cols], summed[:, cols:])
    sent = jnp.where(yhi == 0, summed[:, cols:], summed[:, :cols])
    smoothed = (kept + lax.ppermute(sent, "yh", [(0, 1), (1, 0)]))[:, None, :]

    moved = lax.all_to_all(output.astype(bf16), GROUP, 0, 0, tiled=True)
    features = assemble(moved).reshape(patches, 1, 1, width)
    return features, smoothed


def solution(mesh):
    fine = Mesh(mesh.devices.reshape(4, 2, 2, 2, 4), AXES)
    placed = (
        P(MP, None, None),
        P(MP, DP, None, None),
        P(None, DP),
        P(),
        P(),
        P(None, None, MP),
        P(),
        P(),
        P(MP, None),
    )
    return jax.shard_map(
        block,
        mesh=fine,
        in_specs=placed,
        out_specs=(P(None, DP, MP, None), P(None, MP, DP)),
        check_vma=False,
    )
```

```python
import jax
import jax.numpy as jnp
from jax import lax
from jax.experimental import pallas as pl
from jax.experimental.pallas import tpu as pltpu
from jax.sharding import Mesh
from jax.sharding import PartitionSpec as P


HEAD_DIM = 128
epsilon = 1e-06
bf16 = jnp.bfloat16
f32 = jnp.float32

AXES = ("x", "yh", "core", "yl", "z")
GROUP = ("x", "core")
DP = ("x", "yh", "core")
MP = ("yl", "z")
PIECES = 16
ROWS = 48
PIX_ROWS = 13 * ROWS
LHS_ROWS = 640


def device_id(xc, yh, m):
    return (((xc // 2) * 2 + yh) * 2 + xc % 2) * 8 + m


def everyone():
    return [(xc, yh, m) for xc in range(8) for yh in range(2) for m in range(8)]


NEAR = [
    [device_id(2 * x + c, yh, ((yh ^ s) * 4 + z)) for x in range(4) for yh in range(2) for c in range(2)]
    for s in range(2)
    for z in range(4)
]
HOLDERS = [
    [device_id(xc, yh, 2 * x + c) for x in range(4) for yh in range(2) for c in range(2)] for xc in range(8)
]


def send(array, target):
    pairs = [(device_id(*s), device_id(*target(*s))) for s in everyone()]
    return lax.ppermute(array, AXES, pairs)


def padded(rows, count):
    return jnp.pad(rows, ((0, count - rows.shape[0]), (0, 0)))


def dot(left, right, dims):
    return lax.dot_general(left, right, (dims, ((), ())), preferred_element_type=f32)


def join_kernel(rows_ref, gain_ref, qkv_ref, out_ref, mean_ref, acc_ref):
    step = pl.program_id(0)
    shares, _, cols = rows_ref.shape

    @pl.when(step == 0)
    def _():
        total = jnp.zeros((ROWS, HEAD_DIM), f32)
        for k in range(shares):
            for j in range(cols // HEAD_DIM):
                total += rows_ref[k, :, j * HEAD_DIM : (j + 1) * HEAD_DIM].astype(f32)
        mean = jnp.sum(total, axis=1, keepdims=True) * (1.0 / (shares * cols))
        mean_ref[...] = jnp.broadcast_to(mean, (ROWS, HEAD_DIM))
        acc_ref[...] = jnp.zeros_like(acc_ref)

    per_step = qkv_ref.shape[1] // cols
    rows = jnp.concatenate([rows_ref[per_step * step + k] for k in range(per_step)], axis=1)
    centred = ((rows.astype(f32) - mean_ref[:, :1]) * gain_ref[...]).astype(bf16)
    qkv = jnp.concatenate([qkv_ref[t] for t in range(3)], axis=1)
    acc_ref[...] += dot(centred, qkv, ((1,), (0,)))

    @pl.when(step == pl.num_programs(0) - 1)
    def _():
        for j in range(acc_ref.shape[1] // HEAD_DIM):
            lanes = slice(j * HEAD_DIM, (j + 1) * HEAD_DIM)
            block = acc_ref[:, lanes]
            if 3 * j < 2 * (acc_ref.shape[1] // HEAD_DIM):
                block = block - jnp.mean(block, axis=1, keepdims=True)
            out_ref[:, lanes] = block.astype(bf16)


def join_weights(rows, gain, qkv):
    shares, _, cols = rows.shape
    width, group_cols = qkv.shape[1:]
    per_step = 2
    return pl.pallas_call(
        join_kernel,
        out_shape=jax.ShapeDtypeStruct((ROWS, 3 * group_cols), bf16),
        grid=(shares // per_step,),
        in_specs=[
            pl.BlockSpec((shares, ROWS, cols), lambda i: (0, 0, 0)),
            pl.BlockSpec((1, per_step * cols), lambda i: (0, i)),
            pl.BlockSpec((3, per_step * cols, group_cols), lambda i: (0, i, 0)),
        ],
        out_specs=pl.BlockSpec((ROWS, 3 * group_cols), lambda i: (0, 0)),
        scratch_shapes=[
            pltpu.VMEM((ROWS, HEAD_DIM), f32),
            pltpu.VMEM((ROWS, 3 * group_cols), f32),
        ],
        cost_estimate=pl.CostEstimate(
            flops=6 * width * ROWS * group_cols,
            transcendentals=0,
            bytes_accessed=6 * width * group_cols,
        ),
        name="join_weights",
    )(rows, gain, qkv)


def head_norm(centred, scale, gain):
    variance = jnp.mean(centred * centred, axis=-1, keepdims=True)
    return (centred * (scale * lax.rsqrt(variance * (scale * scale) + epsilon)) * gain).astype(bf16)


def attention_kernel(
    lhs_ref, query_w_ref, key_w_ref, value_w_ref, query_p_ref, key_p_ref, value_p_ref,
    scale_ref, query_gain_ref, key_gain_ref, out_ref, proj_ref, scale_all,
):
    copies, patches, rows = lhs_ref.shape

    @pl.when(pl.program_id(0) == 0)
    def _():
        shape = (patches, patches)
        diagonal = lax.broadcasted_iota(jnp.int32, shape, 0) == lax.broadcasted_iota(jnp.int32, shape, 1)
        for c in range(copies):
            row = jnp.broadcast_to(scale_ref[c : c + 1, :], shape)
            column = jnp.sum(jnp.where(diagonal, row, 0.0), axis=1, keepdims=True)
            scale_all[c] = jnp.broadcast_to(column, (patches, HEAD_DIM))

    weights = jnp.concatenate([query_w_ref[...], key_w_ref[...], value_w_ref[...]], axis=1)
    proj_ref[...] = dot(lhs_ref[...].reshape(copies * patches, rows), weights, ((1,), (0,)))
    first = PIX_ROWS % query_p_ref.shape[0]
    query_p, key_p, value_p = (
        ref[first : first + patches].astype(f32) for ref in (query_p_ref, key_p_ref, value_p_ref)
    )
    ones = jnp.ones((patches, HEAD_DIM), bf16)
    for c in range(copies):
        here = slice(c * patches, (c + 1) * patches)
        scale = scale_all[c]
        query = head_norm(proj_ref[here, :HEAD_DIM] + query_p, scale, query_gain_ref[...])
        key_vec = head_norm(proj_ref[here, HEAD_DIM : 2 * HEAD_DIM] + key_p, scale, key_gain_ref[...])
        value = ((proj_ref[here, 2 * HEAD_DIM :] + value_p) * scale).astype(bf16)
        exp_scores = jnp.exp(dot(query, key_vec, ((1,), (1,))) * HEAD_DIM ** (-0.5)).astype(bf16)
        mixed = dot(exp_scores, jnp.concatenate([value, ones], axis=1), ((1,), (0,)))
        out_ref[c] = (mixed[:, :HEAD_DIM] / mixed[:, HEAD_DIM:]).astype(bf16)


def attend(lhs, joined, scale, query_gain, key_gain):
    copies, patches, rows = lhs.shape
    group_cols = joined.shape[1] // 3
    heads = group_cols // HEAD_DIM
    tail = 256

    def columns(t, count, block):
        return pl.BlockSpec((count, HEAD_DIM), lambda h: (block, t * heads + h))

    return pl.pallas_call(
        attention_kernel,
        out_shape=jax.ShapeDtypeStruct((copies, patches, group_cols), bf16),
        grid=(heads,),
        in_specs=[
            pl.BlockSpec((copies, patches, rows), lambda h: (0, 0, 0)),
            *[columns(t, rows, 0) for t in range(3)],
            *[columns(t, tail, PIX_ROWS // tail) for t in range(3)],
            pl.BlockSpec((copies, patches), lambda h: (0, 0)),
            pl.BlockSpec((1, HEAD_DIM), lambda h: (0, 0)),
            pl.BlockSpec((1, HEAD_DIM), lambda h: (0, 0)),
        ],
        out_specs=pl.BlockSpec((copies, patches, HEAD_DIM), lambda h: (0, 0, h)),
        scratch_shapes=[
            pltpu.VMEM((copies * patches, 3 * HEAD_DIM), f32),
            pltpu.VMEM((copies, patches, HEAD_DIM), f32),
        ],
        cost_estimate=pl.CostEstimate(
            flops=4 * copies * rows * patches * group_cols * 3,
            transcendentals=copies * patches * group_cols,
            bytes_accessed=20 * copies * patches * group_cols,
        ),
        name="attend",
    )(lhs, *[joined] * 6, scale, query_gain[None], key_gain[None])


def assemble_kernel(in_ref, out_ref, sems):
    shares, _, both = in_ref.shape
    cols = both // 2
    copies = []
    for g in range(shares):
        for yb in range(2):
            start = ((g // 2 * 2 + yb) * 2 + g % 2) * cols
            copies.append(
                pltpu.make_async_copy(
                    in_ref.at[g, :, yb * cols : (yb + 1) * cols],
                    out_ref.at[:, start : start + cols],
                    sems.at[g, yb],
                )
            )
    for copy in copies:
        copy.start()
    for copy in copies:
        copy.wait()


def assemble(moved):
    shares, patches, both = moved.shape
    return pl.pallas_call(
        assemble_kernel,
        out_shape=jax.ShapeDtypeStruct((patches, shares * both), bf16),
        in_specs=[pl.BlockSpec(memory_space=pltpu.VMEM)],
        out_specs=pl.BlockSpec(memory_space=pl.ANY),
        scratch_shapes=[pltpu.SemaphoreType.DMA((shares, 2))],
        name="assemble",
    )(moved)


def block(
    clean_image,
    noise_draw,
    embed_weight,
    position_table,
    norm_gain,
    qkv_weight,
    query_gain,
    key_gain,
    out_weight,
):
    xi, yhi, ci = (lax.axis_index(a) for a in ("x", "yh", "core"))
    patches, width = position_table.shape
    cols = embed_weight.shape[1]

    def my_columns(array):
        start = (xi * 4 + ci) * cols
        return [
            lax.dynamic_slice_in_dim(array, start + yb * 2 * cols, cols, axis=1) for yb in range(2)
        ]

    position_here = lax.dynamic_slice_in_dim(position_table, lax.axis_index(DP) * cols, cols, axis=1)
    rows = [padded(embed_weight, PIX_ROWS), padded(position_here, PIECES * ROWS - PIX_ROWS)]
    rows = jnp.concatenate(rows, axis=0).reshape(PIECES, ROWS, cols)
    rows = lax.all_to_all(rows, AXES, 0, 0, axis_index_groups=NEAR, tiled=True)
    noisy = (clean_image[0].astype(f32) + 0.5 * noise_draw[0, 0].astype(f32)).astype(bf16)
    lhs_own = padded(noisy, LHS_ROWS).T
    out_mine = jnp.concatenate(my_columns(out_weight), axis=1)
    out_mine = jnp.broadcast_to(out_mine[None], (8, *out_mine.shape))
    out_mine, lhs_own, rows, own_weight = lax.optimization_barrier(
        (out_mine, lhs_own, rows, embed_weight)
    )
    lhs = lax.all_gather(lhs_own, GROUP)
    piece = join_weights(rows, norm_gain[None], jnp.transpose(qkv_weight, (1, 0, 2)))
    piece = send(piece, lambda xc, yh, m: (m, yh, xc))
    joined = jnp.broadcast_to(piece[None], (PIECES, *piece.shape))
    joined = lax.all_to_all(joined, AXES, 0, 0, axis_index_groups=HOLDERS, tiled=True)
    joined = joined.reshape(PIECES * ROWS, -1)

    other_weight = send(own_weight, lambda xc, yh, m: (xc, 1 - yh, m ^ 4))
    first = jnp.where(yhi == 0, embed_weight, other_weight)
    second = jnp.where(yhi == 0, other_weight, embed_weight)
    weight_two = jnp.concatenate([first, second], axis=1)
    weight_two = padded(weight_two, LHS_ROWS)
    position_two = jnp.concatenate(my_columns(position_table), axis=1).astype(f32)
    embedded = jnp.einsum("cpk,kd->cpd", lhs, weight_two, preferred_element_type=f32) + position_two

    average = jnp.mean(embedded, axis=-1)
    spread = jnp.mean(jnp.square(embedded - average[..., None]), axis=-1)
    stat = jnp.stack([average, spread])
    stats = [stat]
    for k in range(1, 8):
        stats.append(send(stat, lambda xc, yh, m, k=k: (xc ^ k, yh, m)))
    average = sum(each[0] for each in stats) * 0.125
    spread = sum(each[1] + jnp.square(each[0] - average) for each in stats) * 0.125
    scale = lax.rsqrt(spread + epsilon)

    out_mine, joined = lax.optimization_barrier((out_mine, joined))
    out_all = lax.all_to_all(out_mine, MP, 0, 0, tiled=True)

    head_out = attend(lhs, joined, scale, query_gain, key_gain)
    head_out = head_out.reshape(8 * patches, -1)
    head_all = lax.all_gather(head_out, GROUP)
    attention = jnp.einsum("gtc,gcd->td", head_all, out_all, preferred_element_type=f32)
    output = embedded + attention.reshape(8, patches, 2 * cols)

    summed = jnp.sum(output, axis=0) * (1.0 / 16)
    kept = jnp.where(yhi == 0, summed[:, :cols], summed[:, cols:])
    sent = jnp.where(yhi == 0, summed[:, cols:], summed[:, :cols])
    smoothed = (kept + lax.ppermute(sent, "yh", [(0, 1), (1, 0)]))[:, None, :]

    moved = lax.all_to_all(output.astype(bf16), GROUP, 0, 0, tiled=True)
    features = assemble(moved).reshape(patches, 1, 1, width)
    return features, smoothed


def solution(mesh):
    fine = Mesh(mesh.devices.reshape(4, 2, 2, 2, 4), AXES)
    placed = (
        P(MP, None, None),
        P(MP, DP, None, None),
        P(None, DP),
        P(),
        P(),
        P(None, None, MP),
        P(),
        P(),
        P(MP, None),
    )
    return jax.shard_map(
        block,
        mesh=fine,
        in_specs=placed,
        out_specs=(P(None, DP, MP, None), P(None, MP, DP)),
        check_vma=False,
    )
```

```python
import jax
import jax.numpy as jnp
from jax import lax
from jax.experimental import pallas as pl
from jax.experimental.layout import Layout, with_layout_constraint
from jax.experimental.pallas import tpu as pltpu
from jax.sharding import Mesh
from jax.sharding import PartitionSpec as P


HEAD_DIM = 128
epsilon = 1e-06
bf16 = jnp.bfloat16
f32 = jnp.float32

AXES = ("x", "yh", "core", "yl", "z")
GROUP = ("x", "core")
DP = ("x", "yh", "core")
MP = ("yl", "z")
PIECES = 16
ROWS = 48
PIX_ROWS = 13 * ROWS
LHS_ROWS = 640


def device_id(xc, yh, m):
    return (((xc // 2) * 2 + yh) * 2 + xc % 2) * 8 + m


def everyone():
    return [(xc, yh, m) for xc in range(8) for yh in range(2) for m in range(8)]


NEAR = [
    [device_id(2 * x + c, yh, ((yh ^ s) * 4 + z)) for x in range(4) for yh in range(2) for c in range(2)]
    for s in range(2)
    for z in range(4)
]
HOLDERS = [
    [device_id(xc, yh, 2 * x + c) for x in range(4) for yh in range(2) for c in range(2)] for xc in range(8)
]


def send(array, target):
    pairs = [(device_id(*s), device_id(*target(*s))) for s in everyone()]
    return lax.ppermute(array, AXES, pairs)


def padded(rows, count):
    return jnp.pad(rows, ((0, count - rows.shape[0]), (0, 0)))


def dot(left, right, dims):
    return lax.dot_general(left, right, (dims, ((), ())), preferred_element_type=f32)


def join_kernel(rows_ref, gain_ref, qkv_ref, out_ref, mean_ref, acc_ref):
    step = pl.program_id(0)
    shares, _, cols = rows_ref.shape

    @pl.when(step == 0)
    def _():
        total = jnp.zeros((ROWS, HEAD_DIM), f32)
        for k in range(shares):
            for j in range(cols // HEAD_DIM):
                total += rows_ref[k, :, j * HEAD_DIM : (j + 1) * HEAD_DIM].astype(f32)
        mean = jnp.sum(total, axis=1, keepdims=True) * (1.0 / (shares * cols))
        mean_ref[...] = jnp.broadcast_to(mean, (ROWS, HEAD_DIM))
        acc_ref[...] = jnp.zeros_like(acc_ref)

    per_step = qkv_ref.shape[1] // cols
    rows = jnp.concatenate([rows_ref[per_step * step + k] for k in range(per_step)], axis=1)
    centred = ((rows.astype(f32) - mean_ref[:, :1]) * gain_ref[...]).astype(bf16)
    qkv = jnp.concatenate([qkv_ref[t] for t in range(3)], axis=1)
    acc_ref[...] += dot(centred, qkv, ((1,), (0,)))

    @pl.when(step == pl.num_programs(0) - 1)
    def _():
        for j in range(acc_ref.shape[1] // HEAD_DIM):
            lanes = slice(j * HEAD_DIM, (j + 1) * HEAD_DIM)
            block = acc_ref[:, lanes]
            if 3 * j < 2 * (acc_ref.shape[1] // HEAD_DIM):
                block = block - jnp.mean(block, axis=1, keepdims=True)
            out_ref[:, lanes] = block.astype(bf16)


def join_weights(rows, gain, qkv):
    shares, _, cols = rows.shape
    width, group_cols = qkv.shape[1:]
    per_step = 2
    return pl.pallas_call(
        join_kernel,
        out_shape=jax.ShapeDtypeStruct((ROWS, 3 * group_cols), bf16),
        grid=(shares // per_step,),
        in_specs=[
            pl.BlockSpec((shares, ROWS, cols), lambda i: (0, 0, 0)),
            pl.BlockSpec((1, per_step * cols), lambda i: (0, i)),
            pl.BlockSpec((3, per_step * cols, group_cols), lambda i: (0, i, 0)),
        ],
        out_specs=pl.BlockSpec((ROWS, 3 * group_cols), lambda i: (0, 0)),
        scratch_shapes=[
            pltpu.VMEM((ROWS, HEAD_DIM), f32),
            pltpu.VMEM((ROWS, 3 * group_cols), f32),
        ],
        cost_estimate=pl.CostEstimate(
            flops=6 * width * ROWS * group_cols,
            transcendentals=0,
            bytes_accessed=6 * width * group_cols,
        ),
        name="join_weights",
    )(rows, gain, qkv)


def head_norm(centred, scale, gain):
    variance = jnp.mean(centred * centred, axis=-1, keepdims=True)
    return (centred * (scale * lax.rsqrt(variance * (scale * scale) + epsilon)) * gain).astype(bf16)


def attention_kernel(
    lhs_ref, query_w_ref, key_w_ref, value_w_ref, query_p_ref, key_p_ref, value_p_ref,
    scale_ref, query_gain_ref, key_gain_ref, out_ref, proj_ref, scale_all,
):
    copies, patches, rows = lhs_ref.shape

    @pl.when(pl.program_id(0) == 0)
    def _():
        shape = (patches, patches)
        diagonal = lax.broadcasted_iota(jnp.int32, shape, 0) == lax.broadcasted_iota(jnp.int32, shape, 1)
        for c in range(copies):
            row = jnp.broadcast_to(scale_ref[c : c + 1, :], shape)
            column = jnp.sum(jnp.where(diagonal, row, 0.0), axis=1, keepdims=True)
            scale_all[c] = jnp.broadcast_to(column, (patches, HEAD_DIM))

    weights = jnp.concatenate([query_w_ref[...], key_w_ref[...], value_w_ref[...]], axis=1)
    proj_ref[...] = dot(lhs_ref[...].reshape(copies * patches, rows), weights, ((1,), (0,)))
    first = PIX_ROWS % query_p_ref.shape[0]
    query_p, key_p, value_p = (
        ref[first : first + patches].astype(f32) for ref in (query_p_ref, key_p_ref, value_p_ref)
    )
    ones = jnp.ones((patches, HEAD_DIM), bf16)
    for c in range(copies):
        here = slice(c * patches, (c + 1) * patches)
        scale = scale_all[c]
        query = head_norm(proj_ref[here, :HEAD_DIM] + query_p, scale, query_gain_ref[...])
        key_vec = head_norm(proj_ref[here, HEAD_DIM : 2 * HEAD_DIM] + key_p, scale, key_gain_ref[...])
        value = ((proj_ref[here, 2 * HEAD_DIM :] + value_p) * scale).astype(bf16)
        exp_scores = jnp.exp(dot(query, key_vec, ((1,), (1,))) * HEAD_DIM ** (-0.5)).astype(bf16)
        mixed = dot(exp_scores, jnp.concatenate([value, ones], axis=1), ((1,), (0,)))
        out_ref[c] = (mixed[:, :HEAD_DIM] / mixed[:, HEAD_DIM:]).astype(bf16)


def attend(lhs, joined, scale, query_gain, key_gain):
    copies, patches, rows = lhs.shape
    group_cols = joined.shape[1] // 3
    heads = group_cols // HEAD_DIM
    tail = 256

    def columns(t, count, block):
        return pl.BlockSpec((count, HEAD_DIM), lambda h: (block, t * heads + h))

    return pl.pallas_call(
        attention_kernel,
        out_shape=jax.ShapeDtypeStruct((copies, patches, group_cols), bf16),
        grid=(heads,),
        in_specs=[
            pl.BlockSpec((copies, patches, rows), lambda h: (0, 0, 0)),
            *[columns(t, rows, 0) for t in range(3)],
            *[columns(t, tail, PIX_ROWS // tail) for t in range(3)],
            pl.BlockSpec((copies, patches), lambda h: (0, 0)),
            pl.BlockSpec((1, HEAD_DIM), lambda h: (0, 0)),
            pl.BlockSpec((1, HEAD_DIM), lambda h: (0, 0)),
        ],
        out_specs=pl.BlockSpec((copies, patches, HEAD_DIM), lambda h: (0, 0, h)),
        scratch_shapes=[
            pltpu.VMEM((copies * patches, 3 * HEAD_DIM), f32),
            pltpu.VMEM((copies, patches, HEAD_DIM), f32),
        ],
        cost_estimate=pl.CostEstimate(
            flops=4 * copies * rows * patches * group_cols * 3,
            transcendentals=copies * patches * group_cols,
            bytes_accessed=20 * copies * patches * group_cols,
        ),
        name="attend",
    )(lhs, *[joined] * 6, scale, query_gain[None], key_gain[None])


def assemble_kernel(in_ref, out_ref, sems):
    shares, _, both = in_ref.shape
    cols = both // 2
    copies = []
    for g in range(shares):
        for yb in range(2):
            start = ((g // 2 * 2 + yb) * 2 + g % 2) * cols
            copies.append(
                pltpu.make_async_copy(
                    in_ref.at[g, :, yb * cols : (yb + 1) * cols],
                    out_ref.at[:, start : start + cols],
                    sems.at[g, yb],
                )
            )
    for copy in copies:
        copy.start()
    for copy in copies:
        copy.wait()


def assemble(moved):
    shares, patches, both = moved.shape
    return pl.pallas_call(
        assemble_kernel,
        out_shape=jax.ShapeDtypeStruct((patches, shares * both), bf16),
        in_specs=[pl.BlockSpec(memory_space=pltpu.VMEM)],
        out_specs=pl.BlockSpec(memory_space=pl.ANY),
        scratch_shapes=[pltpu.SemaphoreType.DMA((shares, 2))],
        name="assemble",
    )(moved)


def block(
    clean_image,
    noise_draw,
    embed_weight,
    position_table,
    norm_gain,
    qkv_weight,
    query_gain,
    key_gain,
    out_weight,
):
    xi, yhi, ci = (lax.axis_index(a) for a in ("x", "yh", "core"))
    patches, width = position_table.shape
    cols = embed_weight.shape[1]

    def my_columns(array):
        start = (xi * 4 + ci) * cols
        return [
            lax.dynamic_slice_in_dim(array, start + yb * 2 * cols, cols, axis=1) for yb in range(2)
        ]

    out_near = lax.all_gather(jnp.concatenate(my_columns(out_weight), axis=1), "z")

    position_here = lax.dynamic_slice_in_dim(position_table, lax.axis_index(DP) * cols, cols, axis=1)
    rows = [padded(embed_weight, PIX_ROWS), padded(position_here, PIECES * ROWS - PIX_ROWS)]
    rows = jnp.concatenate(rows, axis=0).reshape(PIECES, ROWS, cols)
    rows = lax.all_to_all(rows, AXES, 0, 0, axis_index_groups=NEAR, tiled=True)
    noisy = (clean_image[0].astype(f32) + 0.5 * noise_draw[0, 0].astype(f32)).astype(bf16)
    lhs_own = with_layout_constraint(padded(noisy, LHS_ROWS).T, Layout((0, 1)))
    lhs_own, rows, own_weight = lax.optimization_barrier((lhs_own, rows, embed_weight))
    lhs = lax.all_gather(lhs_own, GROUP)
    piece = join_weights(rows, norm_gain[None], jnp.transpose(qkv_weight, (1, 0, 2)))
    piece = send(piece, lambda xc, yh, m: (m, yh, xc))
    joined = jnp.broadcast_to(piece[None], (PIECES, *piece.shape))
    joined = lax.all_to_all(joined, AXES, 0, 0, axis_index_groups=HOLDERS, tiled=True)
    joined = joined.reshape(PIECES * ROWS, -1)

    other_weight = send(own_weight, lambda xc, yh, m: (xc, 1 - yh, m ^ 4))
    first = jnp.where(yhi == 0, embed_weight, other_weight)
    second = jnp.where(yhi == 0, other_weight, embed_weight)
    weight_two = jnp.concatenate([first, second], axis=1)
    weight_two = padded(weight_two, LHS_ROWS)
    position_two = jnp.concatenate(my_columns(position_table), axis=1).astype(f32)
    embedded = jnp.einsum("cpk,kd->cpd", lhs, weight_two, preferred_element_type=f32) + position_two

    average = jnp.mean(embedded, axis=-1)
    spread = jnp.mean(jnp.square(embedded - average[..., None]), axis=-1)
    stat = jnp.stack([average, spread])
    for partners in ((1,), (2, 4, 6)):
        stats = [stat]
        for k in partners:
            stats.append(send(stat, lambda xc, yh, m, k=k: (xc ^ k, yh, m)))
        share = 1.0 / len(stats)
        average = sum(each[0] for each in stats) * share
        spread = sum(each[1] + jnp.square(each[0] - average) for each in stats) * share
        stat = jnp.stack([average, spread])
    scale = lax.rsqrt(spread + epsilon)

    head_out = attend(lhs, joined, scale, query_gain, key_gain)
    head_out = head_out.reshape(8 * patches, -1)
    head_all = lax.all_gather(head_out, GROUP)

    out_near, _ = lax.optimization_barrier((out_near, head_out))
    out_far = send(out_near, lambda xc, yh, m: (xc, yh ^ (xc & 1), m ^ 4))

    low = lax.axis_index("yl") == 0
    out_all = jnp.concatenate(
        [jnp.where(low, out_near, out_far), jnp.where(low, out_far, out_near)], axis=0
    )
    out_all = lax.optimization_barrier(out_all)
    attention = jnp.einsum("gtc,gcd->td", head_all, out_all, preferred_element_type=f32)
    output = embedded + attention.reshape(8, patches, 2 * cols)

    summed = jnp.sum(output, axis=0) * (1.0 / 16)
    kept = jnp.where(yhi == 0, summed[:, :cols], summed[:, cols:])
    sent = jnp.where(yhi == 0, summed[:, cols:], summed[:, :cols])
    smoothed = (kept + lax.ppermute(sent, "yh", [(0, 1), (1, 0)]))[:, None, :]

    moved = lax.all_to_all(output.astype(bf16), GROUP, 0, 0, tiled=True)
    features = assemble(moved).reshape(patches, 1, 1, width)
    return features, smoothed


def solution(mesh):
    fine = Mesh(mesh.devices.reshape(4, 2, 2, 2, 4), AXES)
    placed = (
        P(MP, None, None),
        P(MP, DP, None, None),
        P(None, DP),
        P(),
        P(),
        P(None, None, MP),
        P(),
        P(),
        P(MP, None),
    )
    return jax.shard_map(
        block,
        mesh=fine,
        in_specs=placed,
        out_specs=(P(None, DP, MP, None), P(None, MP, DP)),
        check_vma=False,
    )
```

```python
import jax
import jax.numpy as jnp
from jax import lax
from jax.experimental import pallas as pl
from jax.experimental.layout import Layout, with_layout_constraint
from jax.experimental.pallas import tpu as pltpu
from jax.sharding import Mesh
from jax.sharding import PartitionSpec as P


HEAD_DIM = 128
epsilon = 1e-06
bf16 = jnp.bfloat16
f32 = jnp.float32

AXES = ("x", "yh", "core", "yl", "z")
GROUP = ("x", "core")
DP = ("x", "yh", "core")
MP = ("yl", "z")
PIECES = 16
ROWS = 48
PIX_ROWS = 13 * ROWS
LHS_ROWS = 640


def device_id(xc, yh, m):
    return (((xc // 2) * 2 + yh) * 2 + xc % 2) * 8 + m


def everyone():
    return [(xc, yh, m) for xc in range(8) for yh in range(2) for m in range(8)]


NEAR = [
    [device_id(2 * x + c, yh, ((yh ^ s) * 4 + z)) for x in range(4) for yh in range(2) for c in range(2)]
    for s in range(2)
    for z in range(4)
]
HOLDERS = [
    [device_id(xc, yh, 2 * x + c) for x in range(4) for yh in range(2) for c in range(2)] for xc in range(8)
]


def send(array, target):
    pairs = [(device_id(*s), device_id(*target(*s))) for s in everyone()]
    return lax.ppermute(array, AXES, pairs)


def x_partner(k):
    return lambda xc, yh, m: (xc ^ (2 * k), yh, m)


def core_partner(xc, yh, m):
    return xc ^ 1, yh, m


def padded(rows, count):
    return jnp.pad(rows, ((0, count - rows.shape[0]), (0, 0)))


def dot(left, right, dims):
    return lax.dot_general(left, right, (dims, ((), ())), preferred_element_type=f32)


def join_kernel(rows_ref, gain_ref, qkv_ref, out_ref, mean_ref, acc_ref):
    step = pl.program_id(0)
    shares, _, cols = rows_ref.shape

    @pl.when(step == 0)
    def _():
        total = jnp.zeros((ROWS, HEAD_DIM), f32)
        for k in range(shares):
            for j in range(cols // HEAD_DIM):
                total += rows_ref[k, :, j * HEAD_DIM : (j + 1) * HEAD_DIM].astype(f32)
        mean = jnp.sum(total, axis=1, keepdims=True) * (1.0 / (shares * cols))
        mean_ref[...] = jnp.broadcast_to(mean, (ROWS, HEAD_DIM))
        acc_ref[...] = jnp.zeros_like(acc_ref)

    per_step = qkv_ref.shape[1] // cols
    rows = jnp.concatenate([rows_ref[per_step * step + k] for k in range(per_step)], axis=1)
    centred = ((rows.astype(f32) - mean_ref[:, :1]) * gain_ref[...]).astype(bf16)
    qkv = jnp.concatenate([qkv_ref[t] for t in range(3)], axis=1)
    acc_ref[...] += dot(centred, qkv, ((1,), (0,)))

    @pl.when(step == pl.num_programs(0) - 1)
    def _():
        for j in range(acc_ref.shape[1] // HEAD_DIM):
            lanes = slice(j * HEAD_DIM, (j + 1) * HEAD_DIM)
            block = acc_ref[:, lanes]
            if 3 * j < 2 * (acc_ref.shape[1] // HEAD_DIM):
                block = block - jnp.mean(block, axis=1, keepdims=True)
            out_ref[:, lanes] = block.astype(bf16)


def join_weights(rows, gain, qkv):
    shares, _, cols = rows.shape
    width, group_cols = qkv.shape[1:]
    per_step = 2
    return pl.pallas_call(
        join_kernel,
        out_shape=jax.ShapeDtypeStruct((ROWS, 3 * group_cols), bf16),
        grid=(shares // per_step,),
        in_specs=[
            pl.BlockSpec((shares, ROWS, cols), lambda i: (0, 0, 0)),
            pl.BlockSpec((1, per_step * cols), lambda i: (0, i)),
            pl.BlockSpec((3, per_step * cols, group_cols), lambda i: (0, i, 0)),
        ],
        out_specs=pl.BlockSpec((ROWS, 3 * group_cols), lambda i: (0, 0)),
        scratch_shapes=[
            pltpu.VMEM((ROWS, HEAD_DIM), f32),
            pltpu.VMEM((ROWS, 3 * group_cols), f32),
        ],
        cost_estimate=pl.CostEstimate(
            flops=6 * width * ROWS * group_cols,
            transcendentals=0,
            bytes_accessed=6 * width * group_cols,
        ),
        name="join_weights",
    )(rows, gain, qkv)


def head_norm(centred, scale, gain):
    variance = jnp.mean(centred * centred, axis=-1, keepdims=True)
    return (centred * (scale * lax.rsqrt(variance * (scale * scale) + epsilon)) * gain).astype(bf16)


def attention_kernel(
    lhs_ref, query_w_ref, key_w_ref, value_w_ref, query_p_ref, key_p_ref, value_p_ref,
    scale_ref, query_gain_ref, key_gain_ref, out_ref, proj_ref, scale_all,
):
    copies, patches, rows = lhs_ref.shape

    @pl.when(pl.program_id(0) == 0)
    def _():
        shape = (patches, patches)
        diagonal = lax.broadcasted_iota(jnp.int32, shape, 0) == lax.broadcasted_iota(jnp.int32, shape, 1)
        for c in range(copies):
            row = jnp.broadcast_to(scale_ref[c : c + 1, :], shape)
            column = jnp.sum(jnp.where(diagonal, row, 0.0), axis=1, keepdims=True)
            scale_all[c] = jnp.broadcast_to(column, (patches, HEAD_DIM))

    weights = jnp.concatenate([query_w_ref[...], key_w_ref[...], value_w_ref[...]], axis=1)
    proj_ref[...] = dot(lhs_ref[...].reshape(copies * patches, rows), weights, ((1,), (0,)))
    first = PIX_ROWS % query_p_ref.shape[0]
    query_p, key_p, value_p = (
        ref[first : first + patches].astype(f32) for ref in (query_p_ref, key_p_ref, value_p_ref)
    )
    ones = jnp.ones((patches, HEAD_DIM), bf16)
    for c in range(copies):
        here = slice(c * patches, (c + 1) * patches)
        scale = scale_all[c]
        query = head_norm(proj_ref[here, :HEAD_DIM] + query_p, scale, query_gain_ref[...])
        key_vec = head_norm(proj_ref[here, HEAD_DIM : 2 * HEAD_DIM] + key_p, scale, key_gain_ref[...])
        value = ((proj_ref[here, 2 * HEAD_DIM :] + value_p) * scale).astype(bf16)
        exp_scores = jnp.exp(dot(query, key_vec, ((1,), (1,))) * HEAD_DIM ** (-0.5)).astype(bf16)
        mixed = dot(exp_scores, jnp.concatenate([value, ones], axis=1), ((1,), (0,)))
        out_ref[c] = (mixed[:, :HEAD_DIM] / mixed[:, HEAD_DIM:]).astype(bf16)


def attend(lhs, joined, scale, query_gain, key_gain):
    copies, patches, rows = lhs.shape
    group_cols = joined.shape[1] // 3
    heads = group_cols // HEAD_DIM
    tail = 256

    def columns(t, count, block):
        return pl.BlockSpec((count, HEAD_DIM), lambda h: (block, t * heads + h))

    return pl.pallas_call(
        attention_kernel,
        out_shape=jax.ShapeDtypeStruct((copies, patches, group_cols), bf16),
        grid=(heads,),
        in_specs=[
            pl.BlockSpec((copies, patches, rows), lambda h: (0, 0, 0)),
            *[columns(t, rows, 0) for t in range(3)],
            *[columns(t, tail, PIX_ROWS // tail) for t in range(3)],
            pl.BlockSpec((copies, patches), lambda h: (0, 0)),
            pl.BlockSpec((1, HEAD_DIM), lambda h: (0, 0)),
            pl.BlockSpec((1, HEAD_DIM), lambda h: (0, 0)),
        ],
        out_specs=pl.BlockSpec((copies, patches, HEAD_DIM), lambda h: (0, 0, h)),
        scratch_shapes=[
            pltpu.VMEM((copies * patches, 3 * HEAD_DIM), f32),
            pltpu.VMEM((copies, patches, HEAD_DIM), f32),
        ],
        cost_estimate=pl.CostEstimate(
            flops=4 * copies * rows * patches * group_cols * 3,
            transcendentals=copies * patches * group_cols,
            bytes_accessed=20 * copies * patches * group_cols,
        ),
        name="attend",
    )(lhs, *[joined] * 6, scale, query_gain[None], key_gain[None])


def assemble_kernel(in_ref, out_ref, sems):
    shares, _, both = in_ref.shape
    cols = both // 2
    copies = []
    for g in range(shares):
        for yb in range(2):
            start = ((g // 2 * 2 + yb) * 2 + g % 2) * cols
            copies.append(
                pltpu.make_async_copy(
                    in_ref.at[g, :, yb * cols : (yb + 1) * cols],
                    out_ref.at[:, start : start + cols],
                    sems.at[g, yb],
                )
            )
    for copy in copies:
        copy.start()
    for copy in copies:
        copy.wait()


def assemble(moved):
    shares, patches, both = moved.shape
    return pl.pallas_call(
        assemble_kernel,
        out_shape=jax.ShapeDtypeStruct((patches, shares * both), bf16),
        in_specs=[pl.BlockSpec(memory_space=pltpu.VMEM)],
        out_specs=pl.BlockSpec(memory_space=pl.ANY),
        scratch_shapes=[pltpu.SemaphoreType.DMA((shares, 2))],
        name="assemble",
    )(moved)


def block(
    clean_image,
    noise_draw,
    embed_weight,
    position_table,
    norm_gain,
    qkv_weight,
    query_gain,
    key_gain,
    out_weight,
):
    xi, yhi, ci = (lax.axis_index(a) for a in ("x", "yh", "core"))
    patches, width = position_table.shape
    cols = embed_weight.shape[1]

    def my_columns(array):
        start = (xi * 4 + ci) * cols
        return [
            lax.dynamic_slice_in_dim(array, start + yb * 2 * cols, cols, axis=1) for yb in range(2)
        ]

    position_here = lax.dynamic_slice_in_dim(position_table, lax.axis_index(DP) * cols, cols, axis=1)
    rows = [padded(embed_weight, PIX_ROWS), padded(position_here, PIECES * ROWS - PIX_ROWS)]
    rows = jnp.concatenate(rows, axis=0).reshape(PIECES, ROWS, cols)
    rows = lax.all_to_all(rows, AXES, 0, 0, axis_index_groups=NEAR, tiled=True)
    noisy = (clean_image[0].astype(f32) + 0.5 * noise_draw[0, 0].astype(f32)).astype(bf16)
    lhs_own = with_layout_constraint(padded(noisy, LHS_ROWS).T, Layout((0, 1)))
    lhs_own = [lhs_own] + [send(lhs_own, x_partner(k)) for k in (1, 2, 3)]

    out_near = jnp.concatenate(my_columns(out_weight), axis=1)
    out_near = [out_near] + [
        send(out_near, lambda xc, yh, m, k=k: (xc, yh, m ^ k)) for k in (1, 2, 3)
    ]

    piece = join_weights(rows, norm_gain[None], jnp.transpose(qkv_weight, (1, 0, 2)))
    lhs_own, own_weight, piece = lax.optimization_barrier((lhs_own, embed_weight, piece))
    piece = send(piece, lambda xc, yh, m: (m, yh, xc))
    other_weight = send(own_weight, lambda xc, yh, m: (xc, 1 - yh, m ^ 4))
    lhs_own = jnp.stack(lhs_own)
    joined = jnp.broadcast_to(piece[None], (PIECES, *piece.shape))
    joined = lax.all_to_all(joined, AXES, 0, 0, axis_index_groups=HOLDERS, tiled=True)
    joined = joined.reshape(PIECES * ROWS, -1)

    lhs_mate = send(lhs_own, core_partner)
    lhs = jnp.zeros((8, patches, LHS_ROWS), bf16)
    for k in range(4):
        lhs = lax.dynamic_update_slice(lhs, lhs_own[k : k + 1], (2 * (xi ^ k) + ci, 0, 0))
        lhs = lax.dynamic_update_slice(lhs, lhs_mate[k : k + 1], (2 * (xi ^ k) + 1 - ci, 0, 0))

    first = jnp.where(yhi == 0, own_weight, other_weight)
    second = jnp.where(yhi == 0, other_weight, own_weight)
    weight_two = jnp.concatenate([first, second], axis=1)
    weight_two = padded(weight_two, LHS_ROWS)
    position_two = jnp.concatenate(my_columns(position_table), axis=1).astype(f32)
    embedded = jnp.einsum("cpk,kd->cpd", lhs, weight_two, preferred_element_type=f32) + position_two

    average = jnp.mean(embedded, axis=-1)
    spread = jnp.mean(jnp.square(embedded - average[..., None]), axis=-1)
    stat = jnp.stack([average, spread])
    for partners in ((1,), (2, 4, 6)):
        stats = [stat]
        for k in partners:
            stats.append(send(stat, lambda xc, yh, m, k=k: (xc ^ k, yh, m)))
        share = 1.0 / len(stats)
        average = sum(each[0] for each in stats) * share
        spread = sum(each[1] + jnp.square(each[0] - average) for each in stats) * share
        stat = jnp.stack([average, spread])
    scale = lax.rsqrt(stat[1] + epsilon)

    out_near, joined = lax.optimization_barrier((jnp.stack(out_near), joined))
    out_far = send(out_near, lambda xc, yh, m: (xc, yh ^ (xc & 1), m ^ 4))

    head_out = attend(lhs, joined, scale, query_gain, key_gain)
    head_out = head_out.reshape(8 * patches, -1)

    tokens = head_out.shape[0]
    heads = [None] * 8
    heads[0] = head_out
    heads[1] = send(head_out, core_partner)
    heads[2] = send(head_out, x_partner(1))
    heads[6] = send(head_out, x_partner(3))
    relayed = [
        send(heads[6][: tokens // 2], x_partner(1)),
        send(heads[2][tokens // 2 :], x_partner(3)),
    ]
    heads[3] = send(heads[2], core_partner)
    heads[7] = send(heads[6], core_partner)
    mates = [send(half, core_partner) for half in relayed]
    heads[4] = lax.optimization_barrier(jnp.concatenate(relayed, axis=0))
    heads[5] = lax.optimization_barrier(jnp.concatenate(mates, axis=0))

    order = lax.axis_index(MP) ^ (2 * xi + ci)
    out_all = jnp.zeros((8, *out_near.shape[1:]), bf16)
    for k in range(4):
        out_all = lax.dynamic_update_slice(out_all, out_near[k : k + 1], (order ^ k, 0, 0))
        out_all = lax.dynamic_update_slice(out_all, out_far[k : k + 1], (order ^ (4 + k), 0, 0))
    output = embedded.reshape(tokens, 2 * cols)
    for k in (0, 1, 2, 6, 3, 7):
        output = lax.optimization_barrier(output + dot(heads[k], out_all[k], ((1,), (0,))))
    for k in (4, 5):
        output = lax.optimization_barrier(output + dot(heads[k], out_all[k], ((1,), (0,))))
    output = output.reshape(8, patches, 2 * cols)

    summed = jnp.sum(output, axis=0) * (1.0 / 16)
    kept = jnp.where(yhi == 0, summed[:, :cols], summed[:, cols:])
    sent = jnp.where(yhi == 0, summed[:, cols:], summed[:, :cols])
    smoothed = (kept + lax.ppermute(sent, "yh", [(0, 1), (1, 0)]))[:, None, :]

    moved = lax.all_to_all(output.astype(bf16), GROUP, 0, 0, tiled=True)
    features = assemble(moved).reshape(patches, 1, 1, width)
    return features, smoothed


def solution(mesh):
    fine = Mesh(mesh.devices.reshape(4, 2, 2, 2, 4), AXES)
    placed = (
        P(MP, None, None),
        P(MP, DP, None, None),
        P(None, DP),
        P(),
        P(),
        P(None, None, MP),
        P(),
        P(),
        P(MP, None),
    )
    return jax.shard_map(
        block,
        mesh=fine,
        in_specs=placed,
        out_specs=(P(None, DP, MP, None), P(None, MP, DP)),
        check_vma=False,
    )
```

```python
import jax
import jax.numpy as jnp
from jax import lax
from jax.experimental import pallas as pl
from jax.experimental.layout import Layout, with_layout_constraint
from jax.experimental.pallas import tpu as pltpu
from jax.sharding import Mesh
from jax.sharding import PartitionSpec as P


HEAD_DIM = 128
epsilon = 1e-06
bf16 = jnp.bfloat16
f32 = jnp.float32

AXES = ("x", "yh", "core", "yl", "z")
GROUP = ("x", "core")
DP = ("x", "yh", "core")
MP = ("yl", "z")
PIECES = 16
ROWS = 48
PIX_ROWS = 13 * ROWS
LHS_ROWS = 640


def device_id(xc, yh, m):
    return (((xc // 2) * 2 + yh) * 2 + xc % 2) * 8 + m


def everyone():
    return [(xc, yh, m) for xc in range(8) for yh in range(2) for m in range(8)]


NEAR = [
    [device_id(2 * x + c, yh, ((yh ^ s) * 4 + z)) for x in range(4) for yh in range(2) for c in range(2)]
    for s in range(2)
    for z in range(4)
]
HOLDERS = [
    [device_id(xc, yh, 2 * x + c) for x in range(4) for yh in range(2) for c in range(2)] for xc in range(8)
]


def send(array, target):
    pairs = [(device_id(*s), device_id(*target(*s))) for s in everyone()]
    return lax.ppermute(array, AXES, pairs)


def x_partner(k):
    return lambda xc, yh, m: (xc ^ (2 * k), yh, m)


def y_partner(xc, yh, m):
    return xc, yh ^ (xc & 1), m ^ 4


def core_partner(xc, yh, m):
    return xc ^ 1, yh, m


def padded(rows, count):
    return jnp.pad(rows, ((0, count - rows.shape[0]), (0, 0)))


def dot(left, right, dims):
    return lax.dot_general(left, right, (dims, ((), ())), preferred_element_type=f32)


def join_kernel(rows_ref, gain_ref, qkv_ref, out_ref, mean_ref, acc_ref):
    step = pl.program_id(0)
    shares, _, cols = rows_ref.shape

    @pl.when(step == 0)
    def _():
        total = jnp.zeros((ROWS, HEAD_DIM), f32)
        for k in range(shares):
            for j in range(cols // HEAD_DIM):
                total += rows_ref[k, :, j * HEAD_DIM : (j + 1) * HEAD_DIM].astype(f32)
        mean = jnp.sum(total, axis=1, keepdims=True) * (1.0 / (shares * cols))
        mean_ref[...] = jnp.broadcast_to(mean, (ROWS, HEAD_DIM))
        acc_ref[...] = jnp.zeros_like(acc_ref)

    per_step = qkv_ref.shape[1] // cols
    rows = jnp.concatenate([rows_ref[per_step * step + k] for k in range(per_step)], axis=1)
    centred = ((rows.astype(f32) - mean_ref[:, :1]) * gain_ref[...]).astype(bf16)
    qkv = jnp.concatenate([qkv_ref[t] for t in range(3)], axis=1)
    acc_ref[...] += dot(centred, qkv, ((1,), (0,)))

    @pl.when(step == pl.num_programs(0) - 1)
    def _():
        for j in range(acc_ref.shape[1] // HEAD_DIM):
            lanes = slice(j * HEAD_DIM, (j + 1) * HEAD_DIM)
            block = acc_ref[:, lanes]
            if 3 * j < 2 * (acc_ref.shape[1] // HEAD_DIM):
                block = block - jnp.mean(block, axis=1, keepdims=True)
            out_ref[:, lanes] = block.astype(bf16)


def join_weights(rows, gain, qkv):
    shares, _, cols = rows.shape
    width, group_cols = qkv.shape[1:]
    per_step = 4
    return pl.pallas_call(
        join_kernel,
        out_shape=jax.ShapeDtypeStruct((ROWS, 3 * group_cols), bf16),
        grid=(shares // per_step,),
        in_specs=[
            pl.BlockSpec((shares, ROWS, cols), lambda i: (0, 0, 0)),
            pl.BlockSpec((1, per_step * cols), lambda i: (0, i)),
            pl.BlockSpec((3, per_step * cols, group_cols), lambda i: (0, i, 0)),
        ],
        out_specs=pl.BlockSpec((ROWS, 3 * group_cols), lambda i: (0, 0)),
        scratch_shapes=[
            pltpu.VMEM((ROWS, HEAD_DIM), f32),
            pltpu.VMEM((ROWS, 3 * group_cols), f32),
        ],
        cost_estimate=pl.CostEstimate(
            flops=6 * width * ROWS * group_cols,
            transcendentals=0,
            bytes_accessed=6 * width * group_cols,
        ),
        name="join_weights",
    )(rows, gain, qkv)


def head_norm(centred, scale, gain):
    variance = jnp.mean(centred * centred, axis=-1, keepdims=True)
    return (centred * (scale * lax.rsqrt(variance * (scale * scale) + epsilon)) * gain).astype(bf16)


def attention_kernel(
    lhs_ref, query_w_ref, key_w_ref, value_w_ref, query_p_ref, key_p_ref, value_p_ref,
    scale_ref, query_gain_ref, key_gain_ref, first_ref, second_ref, proj_ref, scale_all,
):
    copies, patches, rows = lhs_ref.shape

    @pl.when(pl.program_id(0) == 0)
    def _():
        shape = (patches, patches)
        diagonal = lax.broadcasted_iota(jnp.int32, shape, 0) == lax.broadcasted_iota(jnp.int32, shape, 1)
        for c in range(copies):
            row = jnp.broadcast_to(scale_ref[c : c + 1, :], shape)
            column = jnp.sum(jnp.where(diagonal, row, 0.0), axis=1, keepdims=True)
            scale_all[c] = jnp.broadcast_to(column, (patches, HEAD_DIM))

    weights = jnp.concatenate([query_w_ref[...], key_w_ref[...], value_w_ref[...]], axis=1)
    proj_ref[...] = dot(lhs_ref[...].reshape(copies * patches, rows), weights, ((1,), (0,)))
    first = PIX_ROWS % query_p_ref.shape[0]
    query_p, key_p, value_p = (
        ref[first : first + patches].astype(f32) for ref in (query_p_ref, key_p_ref, value_p_ref)
    )
    ones = jnp.ones((patches, HEAD_DIM), bf16)
    for c in range(copies):
        here = slice(c * patches, (c + 1) * patches)
        scale = scale_all[c]
        query = head_norm(proj_ref[here, :HEAD_DIM] + query_p, scale, query_gain_ref[...])
        key_vec = head_norm(proj_ref[here, HEAD_DIM : 2 * HEAD_DIM] + key_p, scale, key_gain_ref[...])
        value = ((proj_ref[here, 2 * HEAD_DIM :] + value_p) * scale).astype(bf16)
        exp_scores = jnp.exp(dot(query, key_vec, ((1,), (1,))) * HEAD_DIM ** (-0.5)).astype(bf16)
        mixed = dot(exp_scores, jnp.concatenate([value, ones], axis=1), ((1,), (0,)))
        out_ref = first_ref if c < copies // 2 else second_ref
        out_ref[c % (copies // 2)] = (mixed[:, :HEAD_DIM] / mixed[:, HEAD_DIM:]).astype(bf16)


def attend(lhs, joined, scale, query_gain, key_gain):
    copies, patches, rows = lhs.shape
    group_cols = joined.shape[1] // 3
    heads = group_cols // HEAD_DIM
    tail = 256

    def columns(t, count, block):
        return pl.BlockSpec((count, HEAD_DIM), lambda h: (block, t * heads + h))

    return pl.pallas_call(
        attention_kernel,
        out_shape=[jax.ShapeDtypeStruct((copies // 2, patches, group_cols), bf16)] * 2,
        grid=(heads,),
        in_specs=[
            pl.BlockSpec((copies, patches, rows), lambda h: (0, 0, 0)),
            *[columns(t, rows, 0) for t in range(3)],
            *[columns(t, tail, PIX_ROWS // tail) for t in range(3)],
            pl.BlockSpec((copies, patches), lambda h: (0, 0)),
            pl.BlockSpec((1, HEAD_DIM), lambda h: (0, 0)),
            pl.BlockSpec((1, HEAD_DIM), lambda h: (0, 0)),
        ],
        out_specs=[pl.BlockSpec((copies // 2, patches, HEAD_DIM), lambda h: (0, 0, h))] * 2,
        scratch_shapes=[
            pltpu.VMEM((copies * patches, 3 * HEAD_DIM), f32),
            pltpu.VMEM((copies, patches, HEAD_DIM), f32),
        ],
        cost_estimate=pl.CostEstimate(
            flops=4 * copies * rows * patches * group_cols * 3,
            transcendentals=copies * patches * group_cols,
            bytes_accessed=20 * copies * patches * group_cols,
        ),
        name="attend",
    )(lhs, *[joined] * 6, scale, query_gain[None], key_gain[None])


def assemble_kernel(in_ref, out_ref, sems):
    shares, _, both = in_ref.shape
    cols = both // 2
    copies = []
    for g in range(shares):
        for yb in range(2):
            start = ((g // 2 * 2 + yb) * 2 + g % 2) * cols
            copies.append(
                pltpu.make_async_copy(
                    in_ref.at[g, :, yb * cols : (yb + 1) * cols],
                    out_ref.at[:, start : start + cols],
                    sems.at[g, yb],
                )
            )
    for copy in copies:
        copy.start()
    for copy in copies:
        copy.wait()


def assemble(moved):
    shares, patches, both = moved.shape
    return pl.pallas_call(
        assemble_kernel,
        out_shape=jax.ShapeDtypeStruct((patches, shares * both), bf16),
        in_specs=[pl.BlockSpec(memory_space=pltpu.VMEM)],
        out_specs=pl.BlockSpec(memory_space=pl.ANY),
        scratch_shapes=[pltpu.SemaphoreType.DMA((shares, 2))],
        name="assemble",
    )(moved)


def block(
    clean_image,
    noise_draw,
    embed_weight,
    position_table,
    norm_gain,
    qkv_weight,
    query_gain,
    key_gain,
    out_weight,
):
    xi, yhi, ci = (lax.axis_index(a) for a in ("x", "yh", "core"))
    patches, width = position_table.shape
    cols = embed_weight.shape[1]

    def my_columns(array):
        start = (xi * 4 + ci) * cols
        return [
            lax.dynamic_slice_in_dim(array, start + yb * 2 * cols, cols, axis=1) for yb in range(2)
        ]

    position_here = lax.dynamic_slice_in_dim(position_table, lax.axis_index(DP) * cols, cols, axis=1)
    rows = [padded(embed_weight, PIX_ROWS), padded(position_here, PIECES * ROWS - PIX_ROWS)]
    rows = jnp.concatenate(rows, axis=0).reshape(PIECES, ROWS, cols)
    rows = lax.all_to_all(rows, AXES, 0, 0, axis_index_groups=NEAR, tiled=True)
    noisy = (clean_image[0].astype(f32) + 0.5 * noise_draw[0, 0].astype(f32)).astype(bf16)
    lhs_own = with_layout_constraint(padded(noisy, LHS_ROWS).T, Layout((0, 1)))
    lhs_own = [lhs_own] + [send(lhs_own, x_partner(k)) for k in (1, 2, 3)]

    out_near = jnp.concatenate(my_columns(out_weight), axis=1)
    out_near = [out_near] + [
        send(out_near, lambda xc, yh, m, k=k: (xc, yh, m ^ k)) for k in (1, 2, 3)
    ]

    piece = join_weights(rows, norm_gain[None], jnp.transpose(qkv_weight, (1, 0, 2)))
    lhs_own, own_weight, piece = lax.optimization_barrier((lhs_own, embed_weight, piece))
    piece = send(piece, lambda xc, yh, m: (m, yh, xc))
    out_far_own = send(out_near[0], y_partner)
    other_weight = send(own_weight, lambda xc, yh, m: (xc, 1 - yh, m ^ 4))
    lhs_own = jnp.stack(lhs_own)
    joined = jnp.broadcast_to(piece[None], (PIECES, *piece.shape))
    joined = lax.all_to_all(joined, AXES, 0, 0, axis_index_groups=HOLDERS, tiled=True)
    joined = joined.reshape(PIECES * ROWS, -1)

    lhs_mate = send(lhs_own, core_partner)
    lhs = jnp.zeros((8, patches, LHS_ROWS), bf16)
    for k in range(4):
        lhs = lax.dynamic_update_slice(lhs, lhs_own[k : k + 1], (2 * (xi ^ k) + ci, 0, 0))
        lhs = lax.dynamic_update_slice(lhs, lhs_mate[k : k + 1], (2 * (xi ^ k) + 1 - ci, 0, 0))

    first = jnp.where(yhi == 0, own_weight, other_weight)
    second = jnp.where(yhi == 0, other_weight, own_weight)
    weight_two = jnp.concatenate([first, second], axis=1)
    weight_two = padded(weight_two, LHS_ROWS)
    position_two = jnp.concatenate(my_columns(position_table), axis=1).astype(f32)
    embedded = [
        jnp.einsum("cpk,kd->cpd", lhs[start : start + 4], weight_two, preferred_element_type=f32)
        + position_two
        for start in (0, 4)
    ]
    averages = [jnp.mean(half, axis=-1) for half in embedded]
    spreads = [
        jnp.mean(jnp.square(half - average[..., None]), axis=-1)
        for half, average in zip(embedded, averages)
    ]
    average, spread = jnp.concatenate(averages, axis=0), jnp.concatenate(spreads, axis=0)
    stat = jnp.stack([average, spread])
    for partners in ((1,), (2, 4, 6)):
        stats = [stat]
        for k in partners:
            stats.append(send(stat, lambda xc, yh, m, k=k: (xc ^ k, yh, m)))
        share = 1.0 / len(stats)
        average = sum(each[0] for each in stats) * share
        spread = sum(each[1] + jnp.square(each[0] - average) for each in stats) * share
        stat = jnp.stack([average, spread])
    scale = lax.rsqrt(stat[1] + epsilon)

    out_rest, joined = lax.optimization_barrier((jnp.stack(out_near[1:]), joined))
    out_far = send(out_rest, y_partner)

    head_out = attend(lhs, joined, scale, query_gain, key_gain)
    tokens = 4 * patches
    top, bottom = (half.reshape(tokens, -1) for half in head_out)

    heads = {(0, 0): top, (0, 1): bottom}
    heads[6, 0] = send(top, x_partner(3))
    heads[2, 1] = send(bottom, x_partner(1))
    heads[2, 0] = send(top, x_partner(1))
    heads[6, 1] = send(bottom, x_partner(3))
    heads[1, 0] = send(top, core_partner)
    heads[1, 1] = send(bottom, core_partner)
    heads[4, 0] = send(heads[6, 0], x_partner(1))
    heads[4, 1] = send(heads[2, 1], x_partner(3))
    for k in (2, 6, 4):
        for half in range(2):
            heads[k + 1, half] = send(heads[k, half], core_partner)

    order = lax.axis_index(MP) ^ (2 * xi + ci)
    out_all = jnp.zeros((8, *out_near[0].shape), bf16)
    for k in range(4):
        far = out_far[k - 1] if k else out_far_own
        out_all = lax.dynamic_update_slice(out_all, out_near[k][None], (order ^ k, 0, 0))
        out_all = lax.dynamic_update_slice(out_all, far[None], (order ^ (4 + k), 0, 0))
    output = [half.reshape(tokens, 2 * cols) for half in embedded]

    def add(half, k):
        grown = output[half] + dot(heads[k, half], out_all[k], ((1,), (0,)))
        output[half] = lax.optimization_barrier(grown)

    for half in range(2):
        for k in (0, 1):
            add(half, k)
    for k in (6, 2):
        for half in (0, 1) if k == 6 else (1, 0):
            add(half, k)
            add(half, k + 1)
    for half in range(2):
        for k in (4, 5):
            add(half, k)
    output = [half.reshape(4, patches, 2 * cols) for half in output]

    summed = (jnp.sum(output[0], axis=0) + jnp.sum(output[1], axis=0)) * (1.0 / 16)
    kept = jnp.where(yhi == 0, summed[:, :cols], summed[:, cols:])
    sent = jnp.where(yhi == 0, summed[:, cols:], summed[:, :cols])
    smoothed = (kept + lax.ppermute(sent, "yh", [(0, 1), (1, 0)]))[:, None, :]

    rounded = jnp.concatenate([half.astype(bf16) for half in output], axis=0)
    moved = lax.all_to_all(rounded, GROUP, 0, 0, tiled=True)
    features = assemble(moved).reshape(patches, 1, 1, width)
    return features, smoothed


def solution(mesh):
    fine = Mesh(mesh.devices.reshape(4, 2, 2, 2, 4), AXES)
    placed = (
        P(MP, None, None),
        P(MP, DP, None, None),
        P(None, DP),
        P(),
        P(),
        P(None, None, MP),
        P(),
        P(),
        P(MP, None),
    )
    return jax.shard_map(
        block,
        mesh=fine,
        in_specs=placed,
        out_specs=(P(None, DP, MP, None), P(None, MP, DP)),
        check_vma=False,
    )
```
